256 devices in a mesh: ctx: 16 (over x, y), head: 16 (over z, core).
Axes of the slice: x: 4, y: 4, z: 8, core: 2. Of those that a mesh axis runs over, the one named last changes fastest.
Arguments:
- tokens: bfloat16 [16384, 4096], P('ctx', 'head'), may hold values from -6 to 6
- doc_ids: int32 [16384], P('ctx'), may hold values from 0 to 7, never falling along the last dimension, each value on 1 to 8192 neighbouring positions
- w_feat: bfloat16 [4096, 1024], P(None, 'head'), may hold values from -0.09375 to 0.09375
- w_value: bfloat16 [4096, 4096], P(None, 'head'), may hold values from -0.09375 to 0.09375
- w_window: bfloat16 [4096, 8192], P(None, 'head'), may hold values from -4 to 4
- w_out: bfloat16 [4096, 4096], P('head'), may hold values from -0.09375 to 0.09375
Outputs:
- layer_out: bfloat16 [16384, 4096], P('ctx', 'head')
The draws below stay inside these ranges and needn't reach their ends.
Inputs may be any that keep to these rules, and one draw needn't show every extreme that they name: `doc_ids`: document ids never fall along the sequence; each of the 8 documents has 1 to 8192 tokens, and one has exactly 8192.
All inputs are finite; a program needn't handle non-finite values.
Results may differ from the reference program's by a relative error of at most 0.019.
Values may be sent and summed in bfloat16 or wider, within the bound.
A program may use at most 128 MiB of HBM per device.

```python
import math
import jax
import jax.numpy as jnp
import numpy as np
from jax import lax

D = 4096
HEADS = 32
HEAD_DIM = 128
FEAT = 16
PHI = 273
WIN = 64
DOCS = 8
TOK_DEV = 1024
TOKENS = 16384
N_CTX = 16


def draw_w_window(key, part):
    first_key = jax.random.fold_in(jax.random.fold_in(key, 17), 0)
    base = jax.random.normal(first_key, (D, HEADS, 2, HEAD_DIM), jnp.float32)
    scaled = (base * D ** (-0.5)).reshape(D, HEADS * 2 * HEAD_DIM)
    return jnp.clip(scaled, -4.0, 4.0).astype(jnp.bfloat16)


def block_levels(key, dims, cuts, smallest, largest):
    loudness = 1.0
    for position, shards_of in cuts:
        steps = jax.random.uniform(jax.random.fold_in(jax.random.fold_in(key, 6), position), (shards_of,), jnp.float32, smallest / len(cuts), largest / len(cuts))
        loudness = loudness * jnp.repeat(jnp.exp(steps), dims[position] // shards_of).reshape((-1,) + (1,) * (len(dims) - 1 - position))
    return loudness


def length_profile(amount, total, most, skew):
    weights = [(1 << 20) // math.isqrt(standing ** skew) + 1 for standing in range(2, amount + 1)]
    surplus, counts = total - most - (amount - 1), [1] * (amount - 1)
    while surplus > 0:
        movable = [i for i in range(amount - 1) if counts[i] < most]
        pool, left = sum([weights[i] for i in movable]), surplus
        for i in movable:
            addition = min(most - counts[i], max(1, left * weights[i] // pool), surplus)
            counts[i] = counts[i] + addition
            surplus = surplus - addition
    return np.array([most] + counts)


def ragged_sizes(stream_key, count, total, reach, lean):
    if count == 2:
        one = jax.random.randint(stream_key, (), max(1, total - reach), min(reach, total - 1) + 1)
        return jnp.stack([one, total - one])
    sizes = jnp.asarray(length_profile(count, total, reach, lean), jnp.int32)
    couples = (count - 1) // 2
    source_of, receiver = sizes[1:1 + 2 * couples:2], sizes[2:2 + 2 * couples:2]
    slack = jnp.minimum(source_of - 1, reach - receiver)
    passed = jax.random.randint(jax.random.fold_in(stream_key, 1), (couples,), 0, 1 << 20) % (slack + 1)
    sizes = sizes.at[1:1 + 2 * couples:2].set(source_of - passed).at[2:2 + 2 * couples:2].set(receiver + passed)
    return sizes[jax.random.permutation(jax.random.fold_in(stream_key, 2), count)]


def noise(key, dims, width, bound, cuts=(), held_as=jnp.bfloat16):
    values = width * jax.random.normal(key, dims, jnp.float32)
    if cuts:
        values = values * block_levels(key, dims, cuts, -0.22, 0.18)
    return jnp.clip(values, -bound, bound).astype(held_as)


def setup_inputs(seed: int = 0) -> dict:
    key_of = jax.random.split(jax.random.key(seed), 7)
    tokens = noise(key_of[0], (TOKENS, D), 1.0, 6.0, ((0, 16), (1, 16)))
    doc_ids = jnp.searchsorted(jnp.cumsum(ragged_sizes(key_of[1], DOCS, TOKENS, TOKENS // 2, 0)), jnp.arange(TOKENS), side="right").astype(jnp.int32)
    w_feat = noise(key_of[2], (D, HEADS * 2 * FEAT), D ** -0.5, 0.09375, ((1, 16),))
    w_value = noise(key_of[3], (D, HEADS * HEAD_DIM), D ** -0.5, 0.09375, ((1, 16),))
    w_window = draw_w_window(jax.random.fold_in(key_of[6], 71), 0)
    w_out = noise(key_of[5], (HEADS * HEAD_DIM, D), (HEADS * HEAD_DIM) ** -0.5, 0.09375, ((0, 16),))
    return {"tokens": tokens, "doc_ids": doc_ids, "w_feat": w_feat, "w_value": w_value, "w_window": w_window, "w_out": w_out}


def feature_map(projected):
    widened = projected.astype(jnp.float32)
    products = widened[..., :, None] * widened[..., None, :]
    products = products.reshape(widened.shape[:-1] + (FEAT * FEAT,))
    constant_term = jnp.ones(widened.shape[:-1] + (1,), jnp.float32)
    return jnp.concatenate([constant_term, widened * FEAT ** (-0.25), products * (2.0 * FEAT) ** (-0.5)], -1).astype(jnp.bfloat16)

def reference(tokens, doc_ids, w_feat, w_value, w_window, w_out):
    total_rows = tokens.shape[0]
    features = jnp.dot(tokens, w_feat, preferred_element_type=jnp.float32).astype(jnp.bfloat16)
    features = features.reshape(total_rows, HEADS, 2 * FEAT)
    phi_query = feature_map(features[..., :FEAT])
    phi_key = feature_map(features[..., FEAT:])
    values_all = jnp.dot(tokens, w_value, preferred_element_type=jnp.float32).astype(jnp.bfloat16)
    values_all = values_all.reshape(total_rows, HEADS, HEAD_DIM)
    window_proj = jnp.dot(tokens, w_window, preferred_element_type=jnp.float32).astype(jnp.bfloat16)
    window_proj = window_proj.reshape(total_rows, HEADS, 2, HEAD_DIM)
    win_query = window_proj[:, :, 0]
    win_key = window_proj[:, :, 1]

    def blocked(array):
        return array.reshape((N_CTX, TOK_DEV) + array.shape[1:])
    inputs = (blocked(phi_query), blocked(phi_key), blocked(values_all), blocked(win_query), blocked(win_key), blocked(doc_ids))
    positions = jnp.arange(TOK_DEV)
    key_pos = jnp.arange(WIN + TOK_DEV)
    highest = lax.Precision.HIGHEST

    def step_block(carry, block_inputs):
        state, last_doc, tail_key, tail_value, tail_doc = carry
        block_q, block_k, block_v, query_block, key_block, doc_block = block_inputs
        allowed = ((doc_block[:, None] == doc_block[None, :]) & (positions[:, None] >= positions[None, :])).astype(jnp.float32)
        wide_q = block_q.astype(jnp.float32)
        wide_k = block_k.astype(jnp.float32)
        wide_v = block_v.astype(jnp.float32)
        scores = (jnp.einsum('thp,shp->hts', wide_q, wide_k, precision=highest) * allowed[None]).astype(jnp.bfloat16)
        inner = jnp.einsum('hts,shd->thd', scores.astype(jnp.float32), wide_v, precision=highest)
        carried = jnp.einsum('thp,hpd->thd', wide_q, state, precision=highest)
        uses = doc_block == last_doc
        linear_out = inner + jnp.where(uses[:, None, None], carried, jnp.zeros_like(carried))
        keeps = (doc_block == doc_block[-1])[:, None, None]
        kept_keys = jnp.where(keeps, wide_k, jnp.zeros_like(wide_k))
        local_state = jnp.einsum('shp,shd->hpd', kept_keys, wide_v, precision=highest)
        new_state = local_state + jnp.where(last_doc == doc_block[-1], state, jnp.zeros_like(state))
        mean_square = lax.optimization_barrier(jnp.mean(linear_out * linear_out, -1, keepdims=True))
        normed = linear_out * lax.rsqrt(mean_square + 1e-05)
        keys_all = jnp.concatenate([tail_key, key_block], 0).astype(jnp.float32)
        values_cat = jnp.concatenate([tail_value, block_v], 0).astype(jnp.float32)
        docs_cat = jnp.concatenate([tail_doc, doc_block], 0)
        within = (key_pos[None, :] > positions[:, None]) & (key_pos[None, :] <= positions[:, None] + WIN) & (docs_cat[None, :] == doc_block[:, None])
        logits = jnp.einsum('thd,shd->hts', query_block.astype(jnp.float32), keys_all, precision=highest) * HEAD_DIM ** (-0.5)
        logits = jnp.where(within[None], logits, -1e+30)
        top_logit = lax.optimization_barrier(jnp.max(logits, -1, keepdims=True))
        weights = jnp.exp(logits - top_logit) * within[None].astype(jnp.float32)
        probs = (weights / lax.optimization_barrier(jnp.sum(weights, -1, keepdims=True))).astype(jnp.bfloat16)
        window_out = jnp.einsum('hts,shd->thd', probs.astype(jnp.float32), values_cat, precision=highest)
        mixed = (normed + window_out).astype(jnp.bfloat16).reshape(TOK_DEV, HEADS * HEAD_DIM)
        new_carry = (new_state, doc_block[-1], key_block[TOK_DEV - WIN:], block_v[TOK_DEV - WIN:], doc_block[TOK_DEV - WIN:])
        return (new_carry, mixed)
    start_carry = (jnp.zeros((HEADS, PHI, HEAD_DIM), jnp.float32), jnp.array(-1, jnp.int32), jnp.zeros((WIN, HEADS, HEAD_DIM), jnp.bfloat16), jnp.zeros((WIN, HEADS, HEAD_DIM), jnp.bfloat16), jnp.full((WIN,), -1, jnp.int32))
    final_carry, mixed_blocks = lax.scan(step_block, start_carry, inputs)
    mixed_all = mixed_blocks.reshape(total_rows, HEADS * HEAD_DIM)
    return jnp.dot(mixed_all, w_out, preferred_element_type=jnp.float32).astype(jnp.bfloat16)
```

```python
import functools

import jax
import jax.numpy as jnp
import numpy as np
from jax import lax
from jax.experimental import pallas as pl
from jax.experimental.pallas import tpu as pltpu
from jax.sharding import PartitionSpec as P

HEAD_DIM = 128
FEAT = 16
WIN = 64
SUB = 256
PACKED = 160
WIDE = 256
LEAD = 128
F32 = jnp.float32
BF16 = jnp.bfloat16
MESH = pl.DeviceIdType.MESH


def selection_tables():
    first = np.zeros((FEAT, PACKED), np.float32)
    second = np.zeros((FEAT, PACKED), np.float32)
    weight = np.zeros((PACKED,), np.float32)
    for p in range(136):
        i, gap = p % 16, p // 16
        first[i, p] = 1.0
        second[(i + gap) % 16, p] = 1.0
        weight[p] = 1.0 / 32 if gap == 0 else 2.0 / 32
    for i in range(FEAT):
        first[i, 144 + i] = 1.0
        weight[144 + i] = 0.25
    query = np.zeros((2, 2, 4 * FEAT, WIDE), np.float32)
    key = np.zeros((2, 2, PACKED, 4 * FEAT), np.float32)
    pick = np.zeros((2, 2, 4 * FEAT, 128), np.float32)
    for head in range(2):
        at = head * 2 * FEAT
        query[head, 0, at : at + FEAT, :PACKED] = first * weight
        query[head, 1, at : at + FEAT, :PACKED] = second
        key[head, 0, :, at + FEAT : at + 2 * FEAT] = first.T
        key[head, 1, :, at + FEAT : at + 2 * FEAT] = second.T
        pick[head, 0, at : at + FEAT, :FEAT] = np.eye(FEAT)
        pick[head, 1, at + FEAT : at + 2 * FEAT, :FEAT] = np.eye(FEAT)
    return tuple(jnp.asarray(t, BF16) for t in (query, key, pick))


def dot(a, b):
    return lax.dot_general(a, b, (((1,), (0,)), ((), ())), preferred_element_type=F32)


def dot_nt(a, b):
    return lax.dot_general(a, b, (((1,), (1,)), ((), ())), preferred_element_type=F32)


def factor_bias(shape, dim):
    p = lax.broadcasted_iota(jnp.int32, shape, dim)
    one = jnp.where(p == 136, 1.0, 0.0)
    two = jnp.where((p == 136) | ((p >= 144) & (p < 160)), 1.0, 0.0)
    return one, two


def kernel(
    nctx, nz,
    tok, doc, wf_in, wv_in, ww_in, wo_in, query_in, key_in, pick_in,
    out,
    gath, wf, wv, ww, af, av, aw, query_t, key_t, pick_t,
    feat, wq, kcat, vcat, docc, docr, fq, fk, phiq,
    docs, lin, win, st_send, st_recv, st, mix, wo, sbuf, rbuf,
    load_sem, tok_sem, wo_sem, ring_send, ring_recv, par_send, par_recv,
    wo_send, wo_recv, doc_send, doc_recv, st_ssem, st_rsem, tail_send, tail_recv,
    mix_send, mix_recv, rs_send, rs_recv,
):
    n_sub = tok.shape[0] // SUB
    units = n_sub * nz
    rows_total = tok.shape[0]
    b = lax.axis_index("ctx")
    head = lax.axis_index("head")
    z = head // 2
    k = head - 2 * z
    other = 1 - k
    way = 1 - 2 * k
    ahead = lax.rem(z + way + nz, nz) * 2 + k
    behind = lax.rem(z - way + nz, nz) * 2 + k
    partner = z * 2 + other

    def sub_rows(i):
        return pl.ds(pl.multiple_of(i * SUB, SUB), SUB)

    def cols(block):
        return pl.ds(pl.multiple_of(block * 256, 256), 256)

    loads = [
        pltpu.make_async_copy(src, dst, load_sem.at[n])
        for n, (src, dst) in enumerate(
            [(wf_in, wf), (wv_in, wv), (ww_in, ww), (query_in, query_t), (key_in, key_t), (pick_in, pick_t)]
        )
    ]

    def tok_load(i):
        return pltpu.make_async_copy(tok.at[sub_rows(i)], gath.at[k, z, sub_rows(i)], tok_sem.at[i])

    for i in range(n_sub):
        tok_load(i).start()
    for load in loads:
        load.start()

    kcat[0:LEAD, :] = jnp.zeros((LEAD, 256), BF16)
    vcat[0:LEAD, :] = jnp.zeros((LEAD, 256), BF16)

    barrier = pltpu.get_barrier_semaphore()

    def greet(n, carry):
        pl.semaphore_signal(
            barrier, inc=1, device_id={"ctx": lax.rem(b + 1 + n, nctx)}, device_id_type=MESH
        )
        return carry

    for peer in (ahead, behind, partner):
        pl.semaphore_signal(barrier, inc=1, device_id={"head": peer}, device_id_type=MESH)
    lax.fori_loop(0, nctx - 1, greet, 0)
    af[...] = jnp.zeros_like(af)
    av[...] = jnp.zeros_like(av)
    aw[...] = jnp.zeros_like(aw)
    pl.semaphore_wait(barrier, nctx + 2)

    def ring_copy(u):
        s = u // n_sub
        rows = sub_rows(u - s * n_sub)
        src = lax.rem(z - s * way + 2 * nz, nz)
        return pltpu.make_async_remote_copy(
            src_ref=gath.at[k, src, rows],
            dst_ref=gath.at[k, src, rows],
            send_sem=ring_send.at[u],
            recv_sem=ring_recv.at[u],
            device_id={"head": ahead},
            device_id_type=MESH,
        )

    def ring_arrival(u):
        s = u // n_sub
        rows = sub_rows(u - s * n_sub)
        src = lax.rem(z - s * way + 2 * nz, nz)
        slot = gath.at[k, src, rows]
        return pltpu.make_async_remote_copy(
            src_ref=slot,
            dst_ref=slot,
            send_sem=ring_send.at[u - n_sub],
            recv_sem=ring_recv.at[u - n_sub],
            device_id={"head": ahead},
            device_id_type=MESH,
        )

    def par_copy(u, side, turn):
        s = u // n_sub
        rows = sub_rows(u - s * n_sub)
        src = lax.rem(z - s * turn + 2 * nz, nz)
        slot = gath.at[side, src, rows]
        return pltpu.make_async_remote_copy(
            src_ref=slot,
            dst_ref=slot,
            send_sem=par_send.at[u],
            recv_sem=par_recv.at[u],
            device_id={"head": partner},
            device_id_type=MESH,
        )

    def accumulate(u, side, turn):
        s = u // n_sub
        rows = sub_rows(u - s * n_sub)
        src = lax.rem(z - s * turn + 2 * nz, nz)
        x = gath[side, src, rows, :]
        w_rows = cols(src * 2 + side)
        af[rows, :] += dot(x, wf[w_rows, :])
        av[rows, :] += dot(x, wv[w_rows, :])
        aw[rows, :] += dot(x, ww[w_rows, :])

    for i in range(n_sub):
        tok_load(i).wait()
        ring_copy(i).start()
        par_copy(i, k, way).start()

    def doc_copy(c, slot):
        return pltpu.make_async_remote_copy(
            src_ref=doc,
            dst_ref=docs.at[slot],
            send_sem=doc_send.at[c],
            recv_sem=doc_recv.at[slot],
            device_id={"ctx": c},
            device_id_type=MESH,
        )

    def wo_copy(d, side, target):
        return pltpu.make_async_remote_copy(
            src_ref=wo_in.at[:, cols(d * 2 + target)],
            dst_ref=wo.at[side, d],
            send_sem=wo_send.at[d],
            recv_sem=wo_recv.at[d],
            device_id={"head": partner},
            device_id_type=MESH,
        )

    def wo_load(d):
        return pltpu.make_async_copy(wo_in.at[:, cols(d * 2 + k)], wo.at[k, d], wo_sem.at[d])

    def start_doc(c, carry):
        doc_copy(c, b).start()
        return carry

    lax.fori_loop(b + 1, nctx, start_doc, 0)

    def start_wo(d, carry):
        wo_copy(d, k, other).start()
        wo_load(d).start()
        return carry

    lax.fori_loop(0, nz, start_wo, 0)

    for load in loads:
        load.wait()

    lag = 2

    def ring_step(u, carry):
        @pl.when((u >= n_sub) & (u < units))
        def _():
            ring_arrival(u).wait_recv()

            @pl.when(u < units - n_sub)
            def _():
                ring_copy(u).start()

            par_copy(u, k, way).start()

        @pl.when(u < units)
        def _():
            accumulate(u, k, way)

        @pl.when(u >= lag)
        def _():
            par_copy(u - lag, other, -way).wait_recv()
            accumulate(u - lag, other, -way)

        return carry

    lax.fori_loop(0, units + lag, ring_step, 0)

    def round_rows(i, carry):
        rows = sub_rows(i)
        late = pl.ds(pl.multiple_of(LEAD + i * SUB, 128), SUB)
        feat[rows, :] = af[rows, :].astype(BF16)
        vcat[late, :] = av[rows, :].astype(BF16)
        wq[rows, 0:128] = aw[rows, 0:128].astype(BF16)
        kcat[late, 0:128] = aw[rows, 128:256].astype(BF16)
        wq[rows, 128:256] = aw[rows, 256:384].astype(BF16)
        kcat[late, 128:256] = aw[rows, 384:512].astype(BF16)
        return carry

    lax.fori_loop(0, n_sub, round_rows, 0)

    def tail_copy(n):
        buf = (kcat, vcat)[n]
        return pltpu.make_async_remote_copy(
            src_ref=buf.at[LEAD + rows_total - WIN : LEAD + rows_total],
            dst_ref=buf.at[LEAD - WIN : LEAD],
            send_sem=tail_send.at[n],
            recv_sem=tail_recv.at[n],
            device_id={"ctx": lax.rem(b + 1, nctx)},
            device_id_type=MESH,
        )

    mine = doc[...].astype(F32)
    first_doc = mine[0:1, 0:1]
    last_doc = mine[7:8, 127:128]
    for i in range(8):
        row = mine[i : i + 1, :]
        docr[0:1, LEAD + i * 128 : LEAD + (i + 1) * 128] = row
        docc[i * 128 : (i + 1) * 128, :] = jnp.broadcast_to(row, (128, 128)).T

    one_k, two_k = factor_bias((PACKED, 1), 0)
    keeps = docr[0:1, LEAD : LEAD + rows_total] == last_doc
    for j in range(2):
        left = dot_nt(key_t[j, 0], feat[...]) + one_k
        right = dot_nt(key_t[j, 1], feat[...]) + two_k
        phi_k = jnp.where(keeps, left * right, 0.0).astype(BF16)
        st_send[j] = dot(phi_k, vcat[LEAD : LEAD + rows_total, j * 128 : (j + 1) * 128]).astype(BF16)

    def st_copy(c, slot):
        return pltpu.make_async_remote_copy(
            src_ref=st_send,
            dst_ref=st_recv.at[slot],
            send_sem=st_ssem.at[c],
            recv_sem=st_rsem.at[slot],
            device_id={"ctx": c},
            device_id_type=MESH,
        )

    @pl.when(b < nctx - 1)
    def _():
        tail_copy(0).start()
        tail_copy(1).start()

    def start_state(c, carry):
        st_copy(c, b).start()
        return carry

    lax.fori_loop(b + 1, nctx, start_state, 0)

    one_q, two_q = factor_bias((1, WIDE), 1)

    def query_rows(i, carry):
        rows = sub_rows(i)
        x = feat[rows, :]
        for j in range(2):
            left = dot(x, query_t[j, 0]) + one_q
            right = dot(x, query_t[j, 1]) + two_q
            phiq[j, rows, :] = (left * right).astype(BF16)
            fq[j, rows, :] = dot(x, pick_t[j, 0]).astype(BF16)
            fk[j, rows, :] = dot(x, pick_t[j, 1]).astype(BF16)
        return carry

    lax.fori_loop(0, n_sub, query_rows, 0)

    for i in range(n_sub):
        lo, hi = i * SUB, (i + 1) * SUB
        t_pos = lax.broadcasted_iota(jnp.int32, (SUB, hi), 0) + lo
        s_pos = lax.broadcasted_iota(jnp.int32, (SUB, hi), 1)
        allowed = (s_pos <= t_pos) & (docc[lo:hi, 0:1] == docr[0:1, LEAD : LEAD + hi])
        for j in range(2):
            d = dot_nt(fq[j, lo:hi, :], fk[j, 0:hi, :])
            taylor = jnp.where(allowed, 1.0 + d * (0.25 + d * 0.03125), 0.0).astype(BF16)
            lin[lo:hi, j * 128 : (j + 1) * 128] = dot(
                taylor, vcat[LEAD : LEAD + hi, j * 128 : (j + 1) * 128]
            )

    def wait_doc(c, carry):
        doc_copy(b, c).wait_recv()
        return carry

    lax.fori_loop(0, b, wait_doc, 0)

    @pl.when(b == 0)
    def _():
        docr[0:1, 0:LEAD] = jnp.full((1, LEAD), -1.0, F32)

    @pl.when(b > 0)
    def _():
        tail_copy(0).wait_recv()
        tail_copy(1).wait_recv()
        docr[0:1, 0:LEAD] = docs[b - 1][7:8, :].astype(F32)

    reach = LEAD + SUB
    gap = lax.broadcasted_iota(jnp.int32, (SUB, reach), 1) - lax.broadcasted_iota(
        jnp.int32, (SUB, reach), 0
    )
    band = (gap > LEAD - WIN) & (gap <= LEAD)
    for i in range(n_sub):
        lo, hi = i * SUB, (i + 1) * SUB
        within = band & (docc[lo:hi, 0:1] == docr[0:1, lo : lo + reach])
        for j in range(2):
            at = slice(j * 128, (j + 1) * 128)
            logits = dot_nt(wq[lo:hi, at], kcat[lo : lo + reach, at]) * HEAD_DIM ** (-0.5)
            logits = jnp.where(within, logits, -1e30)
            top = jnp.max(logits, -1, keepdims=True)
            weights = jnp.where(within, jnp.exp(logits - top), 0.0)
            probs = (weights / jnp.sum(weights, -1, keepdims=True)).astype(BF16)
            win[lo:hi, at] = dot(probs, vcat[lo : lo + reach, at])

    def add_state(c, sums):
        st_copy(b, c).wait_recv()
        same = docs[c][7:8, 127:128].astype(F32) == first_doc
        return sums + jnp.where(same[None], st_recv[c].astype(F32), 0.0)

    total = lax.fori_loop(0, b, add_state, jnp.zeros((2, PACKED, 128), F32))
    st[:, 0:PACKED, :] = total.astype(BF16)
    st[:, PACKED:WIDE, :] = jnp.zeros((2, WIDE - PACKED, 128), BF16)

    def mix_copy(i, side):
        slot = mix.at[side, sub_rows(i)]
        return pltpu.make_async_remote_copy(
            src_ref=slot,
            dst_ref=slot,
            send_sem=mix_send.at[i],
            recv_sem=mix_recv.at[i],
            device_id={"head": partner},
            device_id_type=MESH,
        )

    def mix_rows(i, carry):
        rows = sub_rows(i)
        uses = docc[rows, :] == first_doc
        for j in range(2):
            at = slice(j * 128, (j + 1) * 128)
            carried = dot(phiq[j, rows, :], st[j])
            linear = lin[rows, at] + jnp.where(uses, carried, 0.0)
            square = jnp.mean(linear * linear, -1, keepdims=True)
            normed = linear * lax.rsqrt(square + 1e-5)
            mix[k, rows, at] = (normed + win[rows, at]).astype(BF16)
        mix_copy(i, k).start()
        return carry

    lax.fori_loop(0, n_sub, mix_rows, 0)

    def finish_wo(d, carry):
        wo_load(d).wait()
        wo_copy(d, other, k).wait_recv()
        return carry

    lax.fori_loop(0, nz, finish_wo, 0)

    def sum_copy(u):
        s = u // n_sub
        i = u - s * n_sub
        return pltpu.make_async_remote_copy(
            src_ref=sbuf.at[s, i],
            dst_ref=rbuf.at[s, i],
            send_sem=rs_send.at[u],
            recv_sem=rs_recv.at[u],
            device_id={"head": ahead},
            device_id_type=MESH,
        )

    def sum_step(u, carry):
        s = u // n_sub
        i = u - s * n_sub
        rows = sub_rows(i)
        dest = lax.rem(z - (s + 1) * way + 2 * nz, nz)

        @pl.when(u < n_sub)
        def _():
            mix_copy(i, other).wait_recv()

        part = dot(mix[0, rows, :], wo[0, dest]) + dot(mix[1, rows, :], wo[1, dest])

        @pl.when(u < n_sub)
        def _():
            sbuf[s, i] = part.astype(BF16)
            sum_copy(u).start()

        @pl.when(u >= n_sub)
        def _():
            sum_copy(u - n_sub).wait_recv()
            both = (part + rbuf[s - 1, i].astype(F32)).astype(BF16)

            @pl.when(u < units - n_sub)
            def _():
                sbuf[s, i] = both
                sum_copy(u).start()

            @pl.when(u >= units - n_sub)
            def _():
                out[rows, :] = both

        return carry

    lax.fori_loop(0, units, sum_step, 0)

    def drain_ring(u, carry):
        @pl.when(u < units - n_sub)
        def _():
            ring_copy(u).wait_send()
            sum_copy(u).wait_send()

        par_copy(u, k, way).wait_send()
        return carry

    lax.fori_loop(0, units, drain_ring, 0)

    def drain_later(c, carry):
        doc_copy(c, b).wait_send()
        st_copy(c, b).wait_send()
        return carry

    lax.fori_loop(b + 1, nctx, drain_later, 0)

    @pl.when(b < nctx - 1)
    def _():
        tail_copy(0).wait_send()
        tail_copy(1).wait_send()

    for i in range(n_sub):
        mix_copy(i, k).wait_send()

    def drain_wo(d, carry):
        wo_copy(d, k, other).wait_send()
        return carry

    lax.fori_loop(0, nz, drain_wo, 0)


def solution(mesh):
    nctx, nhead = mesh.shape["ctx"], mesh.shape["head"]
    nz = nhead // 2

    def shards(tokens, doc_ids, w_feat, w_value, w_window, w_out):
        rows = tokens.shape[0]
        width = w_feat.shape[0]
        n_sub = rows // SUB
        units = n_sub * nz
        dma = pltpu.SemaphoreType.DMA
        vmem = pltpu.VMEM
        any_space = pl.BlockSpec(memory_space=pl.ANY)
        vmem_space = pl.BlockSpec(memory_space=pltpu.VMEM)
        query, key, pick = selection_tables()
        return pl.pallas_call(
            functools.partial(kernel, nctx, nz),
            out_shape=jax.ShapeDtypeStruct((rows, 256), BF16),
            in_specs=[any_space, vmem_space] + [any_space] * 7,
            out_specs=vmem_space,
            scratch_shapes=[
                vmem((2, nz, rows, 256), BF16),
                vmem((width, 64), BF16),
                vmem((width, 256), BF16),
                vmem((width, 512), BF16),
                vmem((rows, 64), F32),
                vmem((rows, 256), F32),
                vmem((rows, 512), F32),
                vmem(query.shape, BF16),
                vmem(key.shape, BF16),
                vmem(pick.shape, BF16),
                vmem((rows, 64), BF16),
                vmem((rows, 256), BF16),
                vmem((LEAD + rows, 256), BF16),
                vmem((LEAD + rows, 256), BF16),
                vmem((rows, 128), F32),
                vmem((1, LEAD + rows), F32),
                vmem((2, rows, 128), BF16),
                vmem((2, rows, 128), BF16),
                vmem((2, rows, WIDE), BF16),
                vmem((nctx, 8, 128), jnp.int32),
                vmem((rows, 256), F32),
                vmem((rows, 256), F32),
                vmem((2, PACKED, 128), BF16),
                vmem((nctx, 2, PACKED, 128), BF16),
                vmem((2, WIDE, 128), BF16),
                vmem((2, rows, 256), BF16),
                vmem((2, nz, 256, 256), BF16),
                vmem((nz - 1, n_sub, SUB, 256), BF16),
                vmem((nz - 1, n_sub, SUB, 256), BF16),
                dma((6,)),
                dma((n_sub,)),
                dma((nz,)),
                dma((units,)),
                dma((units,)),
                dma((units,)),
                dma((units,)),
                dma((nz,)),
                dma((nz,)),
                dma((nctx,)),
                dma((nctx,)),
                dma((nctx,)),
                dma((nctx,)),
                dma((2,)),
                dma((2,)),
                dma((n_sub,)),
                dma((n_sub,)),
                dma((units,)),
                dma((units,)),
            ],
            compiler_params=pltpu.CompilerParams(
                collective_id=0, has_side_effects=True, vmem_limit_bytes=60 * 1024 * 1024
            ),
            name="based_layer",
        )(
            tokens,
            doc_ids.reshape(8, 128),
            w_feat,
            w_value,
            w_window,
            w_out,
            query,
            key,
            pick,
        )

    return jax.shard_map(
        shards,
        mesh=mesh,
        in_specs=(
            P("ctx", "head"),
            P("ctx"),
            P(None, "head"),
            P(None, "head"),
            P(None, "head"),
            P("head", None),
        ),
        out_specs=P("ctx", "head"),
        check_vma=False,
    )
```

```python
import functools

import jax
import jax.numpy as jnp
import numpy as np
from jax import lax
from jax.experimental import pallas as pl
from jax.experimental.pallas import tpu as pltpu
from jax.sharding import PartitionSpec as P

HEAD_DIM = 128
FEAT = 16
WIN = 64
SUB = 256
WIDE = 256
PART = 32
TABLE = 1536
LEAD = 128
F32 = jnp.float32
BF16 = jnp.bfloat16
MESH = pl.DeviceIdType.MESH


def selection_tables():
    first = np.zeros((FEAT, WIDE), np.float32)
    second = np.zeros((FEAT, WIDE), np.float32)
    weight = np.zeros((WIDE,), np.float32)
    for g in range(8):
        for r in range(FEAT):
            p = g * PART + r
            first[r, p] = 1.0
            second[(r + g) % FEAT, p] = 1.0
            weight[p] = 1.0 / 32 if g == 0 else 2.0 / 32
        p = g * PART + 16
        first[g, p] = 1.0
        second[g + 8, p] = 1.0
        weight[p] = 2.0 / 32
        for n in range(2):
            first[2 * g + n, p + 1 + n] = 1.0
            weight[p + 1 + n] = 0.25
    query = np.zeros((2, 2, 4 * FEAT, WIDE), np.float32)
    key = np.zeros((2, 2, WIDE, 4 * FEAT), np.float32)
    pick = np.zeros((2, 2, 4 * FEAT, 128), np.float32)
    for head in range(2):
        at = head * 2 * FEAT
        query[head, 0, at : at + FEAT] = first * weight
        query[head, 1, at : at + FEAT] = second
        key[head, 0, :, at + FEAT : at + 2 * FEAT] = first.T
        key[head, 1, :, at + FEAT : at + 2 * FEAT] = second.T
        pick[head, 0, at : at + FEAT, :FEAT] = np.eye(FEAT)
        pick[head, 1, at + FEAT : at + 2 * FEAT, :FEAT] = np.eye(FEAT)
    table = np.zeros((TABLE, WIDE), np.float32)
    table[0:256] = query.reshape(256, WIDE)
    table[256:1280, 0 : 4 * FEAT] = key.reshape(4 * WIDE, 4 * FEAT)
    table[1280:1536, 0:128] = pick.reshape(256, 128)
    return jnp.asarray(table, BF16)


def dot(a, b):
    return lax.dot_general(a, b, (((1,), (0,)), ((), ())), preferred_element_type=F32)


def dot_nt(a, b):
    return lax.dot_general(a, b, (((1,), (1,)), ((), ())), preferred_element_type=F32)


def factor_bias(shape, dim):
    p = lax.broadcasted_iota(jnp.int32, shape, dim)
    one = jnp.where(p == 19, 1.0, 0.0)
    two = jnp.where((p == 19) | (p % PART == 17) | (p % PART == 18), 1.0, 0.0)
    return one, two


def kernel(
    nctx, nz,
    tok, doc, wf_in, wv_in, ww_in, wo_in, table_in,
    out,
    gath, wf, wv, ww, af, av, aw, table,
    feat, wq, kcat, vcat, docc, docr, fq, fk, phiq,
    docs, lin, win, st_send, st_recv, st_sums, st, mix, wo, sbuf, rbuf,
    load_sem, tok_sem, wo_sem, ring_send, ring_recv, par_send, par_recv,
    wo_send, wo_recv, doc_send, doc_recv, st_ssem, st_rsem, sum_ssem, sum_rsem, tail_send, tail_recv,
    mix_send, mix_recv, rs_send, rs_recv,
):
    n_sub = tok.shape[0] // SUB
    units = n_sub * nz
    rows_total = tok.shape[0]
    part = WIDE // nctx
    b = lax.axis_index("ctx")
    head = lax.axis_index("head")
    z = head // 2
    k = head - 2 * z
    other = 1 - k
    way = 1 - 2 * k
    ahead = lax.rem(z + way + nz, nz) * 2 + k
    behind = lax.rem(z - way + nz, nz) * 2 + k
    partner = z * 2 + other

    def sub_rows(i):
        return pl.ds(pl.multiple_of(i * SUB, SUB), SUB)

    def cols(block):
        return pl.ds(pl.multiple_of(block * 256, 256), 256)

    def bulk(ref, sem):
        return pltpu.make_async_copy(ref, ref, sem.at[0])

    loads = [
        pltpu.make_async_copy(src, dst, load_sem.at[n])
        for n, (src, dst) in enumerate(
            [(wf_in, wf), (wv_in, wv), (ww_in, ww), (table_in, table)]
        )
    ]

    def tok_load(i):
        return pltpu.make_async_copy(tok.at[sub_rows(i)], gath.at[k, z, sub_rows(i)], tok_sem.at[i])

    for i in range(n_sub):
        tok_load(i).start()
    for load in loads:
        load.start()

    kcat[0:LEAD, :] = jnp.zeros((LEAD, 256), BF16)
    vcat[0:LEAD, :] = jnp.zeros((LEAD, 256), BF16)

    barrier = pltpu.get_barrier_semaphore()

    def greet(n, carry):
        pl.semaphore_signal(
            barrier, inc=1, device_id={"ctx": lax.rem(b + 1 + n, nctx)}, device_id_type=MESH
        )
        return carry

    for peer in (ahead, behind, partner):
        pl.semaphore_signal(barrier, inc=1, device_id={"head": peer}, device_id_type=MESH)
    lax.fori_loop(0, nctx - 1, greet, 0)
    af[...] = jnp.zeros_like(af)
    av[...] = jnp.zeros_like(av)
    aw[...] = jnp.zeros_like(aw)
    pl.semaphore_wait(barrier, nctx + 2)

    def ring_copy(u):
        s = u // n_sub
        rows = sub_rows(u - s * n_sub)
        src = lax.rem(z - s * way + 2 * nz, nz)
        return pltpu.make_async_remote_copy(
            src_ref=gath.at[k, src, rows],
            dst_ref=gath.at[k, src, rows],
            send_sem=ring_send.at[0],
            recv_sem=ring_recv.at[u],
            device_id={"head": ahead},
            device_id_type=MESH,
        )

    def ring_arrival(u):
        s = u // n_sub
        rows = sub_rows(u - s * n_sub)
        src = lax.rem(z - s * way + 2 * nz, nz)
        slot = gath.at[k, src, rows]
        return pltpu.make_async_remote_copy(
            src_ref=slot,
            dst_ref=slot,
            send_sem=ring_send.at[0],
            recv_sem=ring_recv.at[u - n_sub],
            device_id={"head": ahead},
            device_id_type=MESH,
        )

    def par_copy(u, side, turn):
        s = u // n_sub
        rows = sub_rows(u - s * n_sub)
        src = lax.rem(z - s * turn + 2 * nz, nz)
        slot = gath.at[side, src, rows]
        return pltpu.make_async_remote_copy(
            src_ref=slot,
            dst_ref=slot,
            send_sem=par_send.at[0],
            recv_sem=par_recv.at[u],
            device_id={"head": partner},
            device_id_type=MESH,
        )

    def accumulate(u, side, turn):
        s = u // n_sub
        rows = sub_rows(u - s * n_sub)
        src = lax.rem(z - s * turn + 2 * nz, nz)
        x = gath[side, src, rows, :]
        w_rows = cols(src * 2 + side)
        af[rows, :] += dot_nt(x, wf[:, w_rows])
        av[rows, :] += dot(x, wv[w_rows, :])
        aw[rows, :] += dot(x, ww[w_rows, :])

    for i in range(n_sub):
        tok_load(i).wait()
        ring_copy(i).start()
        par_copy(i, k, way).start()

    def doc_copy(c, slot):
        return pltpu.make_async_remote_copy(
            src_ref=doc,
            dst_ref=docs.at[slot],
            send_sem=doc_send.at[0],
            recv_sem=doc_recv.at[0],
            device_id={"ctx": c},
            device_id_type=MESH,
        )

    def wo_copy(d, side, target):
        return pltpu.make_async_remote_copy(
            src_ref=wo_in.at[:, cols(d * 2 + target)],
            dst_ref=wo.at[side, d],
            send_sem=wo_send.at[0],
            recv_sem=wo_recv.at[0],
            device_id={"head": partner},
            device_id_type=MESH,
        )

    def wo_load(d):
        return pltpu.make_async_copy(wo_in.at[:, cols(d * 2 + k)], wo.at[k, d], wo_sem.at[0])

    def start_doc(n, carry):
        doc_copy(lax.rem(b + n, nctx), b).start()
        return carry

    lax.fori_loop(1, nctx, start_doc, 0)

    def start_wo(d, carry):
        wo_copy(d, k, other).start()
        wo_load(d).start()
        return carry

    lax.fori_loop(0, nz, start_wo, 0)

    for load in loads:
        load.wait()

    lag = 2

    def ring_step(u, carry):
        @pl.when((u >= n_sub) & (u < units))
        def _():
            ring_arrival(u).wait_recv()

            @pl.when(u < units - n_sub)
            def _():
                ring_copy(u).start()

            par_copy(u, k, way).start()

        @pl.when(u < units)
        def _():
            accumulate(u, k, way)

        @pl.when(u >= lag)
        def _():
            par_copy(u - lag, other, -way).wait_recv()
            accumulate(u - lag, other, -way)

        return carry

    lax.fori_loop(0, units + lag, ring_step, 0)

    def round_rows(i, carry):
        rows = sub_rows(i)
        late = pl.ds(pl.multiple_of(LEAD + i * SUB, 128), SUB)
        feat[rows, :] = af[rows, :].astype(BF16)
        vcat[late, :] = av[rows, :].astype(BF16)
        wq[rows, 0:128] = aw[rows, 0:128].astype(BF16)
        kcat[late, 0:128] = aw[rows, 128:256].astype(BF16)
        wq[rows, 128:256] = aw[rows, 256:384].astype(BF16)
        kcat[late, 128:256] = aw[rows, 384:512].astype(BF16)
        return carry

    lax.fori_loop(0, n_sub, round_rows, 0)

    def tail_copy(n):
        buf = (kcat, vcat)[n]
        return pltpu.make_async_remote_copy(
            src_ref=buf.at[LEAD + rows_total - WIN : LEAD + rows_total],
            dst_ref=buf.at[LEAD - WIN : LEAD],
            send_sem=tail_send.at[n],
            recv_sem=tail_recv.at[n],
            device_id={"ctx": lax.rem(b + 1, nctx)},
            device_id_type=MESH,
        )

    mine = doc[...].astype(F32)
    last_doc = mine[7:8, 127:128]
    for i in range(8):
        row = mine[i : i + 1, :]
        docr[0:1, LEAD + i * 128 : LEAD + (i + 1) * 128] = row
        docc[i * 128 : (i + 1) * 128, :] = jnp.broadcast_to(row, (128, 128)).T

    one_k, two_k = factor_bias((WIDE, 1), 0)
    keeps = docr[0:1, LEAD : LEAD + rows_total] == last_doc
    for j in range(2):
        at = 256 + 512 * j
        left = dot_nt(table[at : at + 256, 0:64], feat[...]) + one_k
        right = dot_nt(table[at + 256 : at + 512, 0:64], feat[...]) + two_k
        phi_k = jnp.where(keeps, left * right, 0.0).astype(BF16)
        local = dot(phi_k, vcat[LEAD : LEAD + rows_total, j * 128 : (j + 1) * 128])
        st_send[:, j * part : (j + 1) * part, :] = local.astype(BF16).reshape(nctx, part, 128)

    def st_copy(c, slot):
        return pltpu.make_async_remote_copy(
            src_ref=st_send.at[c],
            dst_ref=st_recv.at[slot],
            send_sem=st_ssem.at[0],
            recv_sem=st_rsem.at[0],
            device_id={"ctx": c},
            device_id_type=MESH,
        )

    def start_state(n, carry):
        st_copy(lax.rem(b + n, nctx), b).start()
        return carry

    lax.fori_loop(1, nctx, start_state, 0)

    @pl.when(b < nctx - 1)
    def _():
        tail_copy(0).start()
        tail_copy(1).start()

    one_q, two_q = factor_bias((1, WIDE), 1)

    def query_rows(i, carry):
        rows = sub_rows(i)
        x = feat[rows, :]
        for j in range(2):
            left = dot(x, table[128 * j : 128 * j + 64, :]) + one_q
            right = dot(x, table[128 * j + 64 : 128 * j + 128, :]) + two_q
            phiq[j, rows, :] = (left * right).astype(BF16)
            at = 1280 + 128 * j
            fq[j, rows, :] = dot(x, table[at : at + 64, 0:128]).astype(BF16)
            fk[j, rows, :] = dot(x, table[at + 64 : at + 128, 0:128]).astype(BF16)
        return carry

    lax.fori_loop(0, n_sub, query_rows, 0)

    for i in range(n_sub):
        lo, hi = i * SUB, (i + 1) * SUB
        t_pos = lax.broadcasted_iota(jnp.int32, (SUB, hi), 0) + lo
        s_pos = lax.broadcasted_iota(jnp.int32, (SUB, hi), 1)
        allowed = (s_pos <= t_pos) & (docc[lo:hi, 0:1] == docr[0:1, LEAD : LEAD + hi])
        for j in range(2):
            d = dot_nt(fq[j, lo:hi, :], fk[j, 0:hi, :])
            taylor = jnp.where(allowed, 1.0 + d * (0.25 + d * 0.03125), 0.0).astype(BF16)
            lin[lo:hi, j * 128 : (j + 1) * 128] = dot(
                taylor, vcat[LEAD : LEAD + hi, j * 128 : (j + 1) * 128]
            )

    def sum_back(c, slot):
        return pltpu.make_async_remote_copy(
            src_ref=st_sums.at[c],
            dst_ref=st.at[slot],
            send_sem=sum_ssem.at[0],
            recv_sem=sum_rsem.at[0],
            device_id={"ctx": c},
            device_id_type=MESH,
        )

    bulk(docs.at[0 : nctx - 1], doc_recv).wait()
    bulk(st_recv.at[0 : nctx - 1], st_rsem).wait()
    docs[b] = doc[...]
    st_recv[b] = st_send[b]

    def add_block(c, carry):
        sums, sums_doc = carry
        block_doc = docs[c][7:8, 127:128]
        sums = st_recv[c].astype(F32) + jnp.where(sums_doc == block_doc, sums, 0.0)
        st_sums[c + 1] = sums.astype(BF16)

        @pl.when(c + 1 != b)
        def _():
            sum_back(c + 1, b).start()

        return sums, block_doc

    lax.fori_loop(
        0, nctx - 1, add_block, (jnp.zeros((2 * part, 128), F32), jnp.full((1, 1), -1, jnp.int32))
    )

    @pl.when(b == 0)
    def _():
        docr[0:1, 0:LEAD] = jnp.full((1, LEAD), -1.0, F32)

    @pl.when(b > 0)
    def _():
        tail_copy(0).wait_recv()
        tail_copy(1).wait_recv()
        docr[0:1, 0:LEAD] = docs[b - 1][7:8, :].astype(F32)

    reach = LEAD + SUB
    gap = lax.broadcasted_iota(jnp.int32, (SUB, reach), 1) - lax.broadcasted_iota(
        jnp.int32, (SUB, reach), 0
    )
    band = (gap > LEAD - WIN) & (gap <= LEAD)
    for i in range(n_sub):
        lo, hi = i * SUB, (i + 1) * SUB
        within = band & (docc[lo:hi, 0:1] == docr[0:1, lo : lo + reach])
        for j in range(2):
            at = slice(j * 128, (j + 1) * 128)
            logits = dot_nt(wq[lo:hi, at], kcat[lo : lo + reach, at]) * HEAD_DIM ** (-0.5)
            logits = jnp.where(within, logits, -1e30)
            top = jnp.max(logits, -1, keepdims=True)
            weights = jnp.where(within, jnp.exp(logits - top), 0.0)
            probs = (weights / jnp.sum(weights, -1, keepdims=True)).astype(BF16)
            win[lo:hi, at] = dot(probs, vcat[lo : lo + reach, at])

    @pl.when(b == 0)
    def _():
        st[...] = jnp.zeros_like(st)

    @pl.when(b > 0)
    def _():
        bulk(st.at[0 : nctx - 1], sum_rsem).wait()
        st[b] = st_sums[b]

    state = [
        st[:, j * part : (j + 1) * part, :].reshape(WIDE, 128) for j in range(2)
    ]

    def mix_copy(i, side):
        slot = mix.at[side, sub_rows(i)]
        return pltpu.make_async_remote_copy(
            src_ref=slot,
            dst_ref=slot,
            send_sem=mix_send.at[0],
            recv_sem=mix_recv.at[i],
            device_id={"head": partner},
            device_id_type=MESH,
        )

    def mix_rows(i, carry):
        rows = sub_rows(i)
        uses = docc[rows, :] == docr[0:1, LEAD - 1 : LEAD]
        for j in range(2):
            at = slice(j * 128, (j + 1) * 128)
            carried = dot(phiq[j, rows, :], state[j])
            linear = lin[rows, at] + jnp.where(uses, carried, 0.0)
            square = jnp.mean(linear * linear, -1, keepdims=True)
            normed = linear * lax.rsqrt(square + 1e-5)
            mix[k, rows, at] = (normed + win[rows, at]).astype(BF16)
        mix_copy(i, k).start()
        return carry


    bulk(wo.at[k], wo_sem).wait()
    bulk(wo.at[other], wo_recv).wait()

    def sum_copy(u):
        s = u // n_sub
        i = u - s * n_sub
        return pltpu.make_async_remote_copy(
            src_ref=sbuf.at[s, i],
            dst_ref=rbuf.at[s, i],
            send_sem=rs_send.at[0],
            recv_sem=rs_recv.at[u],
            device_id={"head": ahead},
            device_id_type=MESH,
        )

    def sum_step(u, carry):
        s = u // n_sub
        i = u - s * n_sub
        rows = sub_rows(i)
        dest = lax.rem(z - (s + 1) * way + 2 * nz, nz)

        @pl.when(u < n_sub)
        def _():
            mix_copy(i, other).wait_recv()

        part = dot(mix[0, rows, :], wo[0, dest]) + dot(mix[1, rows, :], wo[1, dest])

        @pl.when(u < n_sub)
        def _():
            sbuf[s, i] = part.astype(BF16)
            sum_copy(u).start()

        @pl.when(u >= n_sub)
        def _():
            sum_copy(u - n_sub).wait_recv()
            both = (part + rbuf[s - 1, i].astype(F32)).astype(BF16)

            @pl.when(u < units - n_sub)
            def _():
                sbuf[s, i] = both
                sum_copy(u).start()

            @pl.when(u >= units - n_sub)
            def _():
                out[rows, :] = both

        return carry

    def first_step(i, carry):
        @pl.when(i < n_sub)
        def _():
            mix_rows(i, 0)

        @pl.when(i > 0)
        def _():
            sum_step(i - 1, 0)

        return carry

    lax.fori_loop(0, n_sub + 1, first_step, 0)
    lax.fori_loop(n_sub, units, sum_step, 0)

    bulk(gath.at[k, 0 : nz - 1], ring_send).wait()
    bulk(gath.at[k], par_send).wait()
    bulk(sbuf, rs_send).wait()
    bulk(docs.at[0 : nctx - 1], doc_send).wait()
    bulk(st_send.at[0 : nctx - 1], st_ssem).wait()
    bulk(mix.at[k], mix_send).wait()
    bulk(wo.at[k], wo_send).wait()

    @pl.when(b == 0)
    def _():
        bulk(st_sums.at[0 : nctx - 1], sum_ssem).wait()

    @pl.when(b > 0)
    def _():
        bulk(st_sums.at[0 : nctx - 2], sum_ssem).wait()

    @pl.when(b < nctx - 1)
    def _():
        tail_copy(0).wait_send()
        tail_copy(1).wait_send()


def solution(mesh):
    nctx, nhead = mesh.shape["ctx"], mesh.shape["head"]
    nz = nhead // 2

    def shards(tokens, doc_ids, w_feat, w_value, w_window, w_out):
        rows = tokens.shape[0]
        width = w_value.shape[0]
        n_sub = rows // SUB
        units = n_sub * nz
        dma = pltpu.SemaphoreType.DMA
        vmem = pltpu.VMEM
        hbm_space = pl.BlockSpec(memory_space=pltpu.HBM)
        vmem_space = pl.BlockSpec(memory_space=pltpu.VMEM)
        return pl.pallas_call(
            functools.partial(kernel, nctx, nz),
            out_shape=jax.ShapeDtypeStruct((rows, 256), BF16),
            in_specs=[hbm_space, vmem_space] + [hbm_space] * 5,
            out_specs=vmem_space,
            scratch_shapes=[
                vmem((2, nz, rows, 256), BF16),
                vmem((64, width), BF16),
                vmem((width, 256), BF16),
                vmem((width, 512), BF16),
                vmem((rows, 64), F32),
                vmem((rows, 256), F32),
                vmem((rows, 512), F32),
                vmem((TABLE, WIDE), BF16),
                vmem((rows, 64), BF16),
                vmem((rows, 256), BF16),
                vmem((LEAD + rows, 256), BF16),
                vmem((LEAD + rows, 256), BF16),
                vmem((rows, 128), F32),
                vmem((1, LEAD + rows), F32),
                vmem((2, rows, 128), BF16),
                vmem((2, rows, 128), BF16),
                vmem((2, rows, WIDE), BF16),
                vmem((nctx, 8, 128), jnp.int32),
                vmem((rows, 256), F32),
                vmem((rows, 256), F32),
                vmem((nctx, 2 * WIDE // nctx, 128), BF16),
                vmem((nctx, 2 * WIDE // nctx, 128), BF16),
                vmem((nctx, 2 * WIDE // nctx, 128), BF16),
                vmem((nctx, 2 * WIDE // nctx, 128), BF16),
                vmem((2, rows, 256), BF16),
                vmem((2, nz, 256, 256), BF16),
                vmem((nz - 1, n_sub, SUB, 256), BF16),
                vmem((nz - 1, n_sub, SUB, 256), BF16),
                dma((4,)),
                dma((n_sub,)),
                dma((1,)),
                dma((1,)),
                dma((units,)),
                dma((1,)),
                dma((units,)),
                dma((1,)),
                dma((1,)),
                dma((1,)),
                dma((1,)),
                dma((1,)),
                dma((1,)),
                dma((1,)),
                dma((1,)),
                dma((2,)),
                dma((2,)),
                dma((1,)),
                dma((n_sub,)),
                dma((1,)),
                dma((units,)),
            ],
            compiler_params=pltpu.CompilerParams(
                collective_id=0, has_side_effects=True, vmem_limit_bytes=67043328 - 600 * 1024
            ),
            name="based_layer",
        )(
            tokens,
            doc_ids.reshape(8, 128),
            w_feat.T,
            w_value,
            w_window,
            w_out,
            selection_tables(),
        )

    return jax.shard_map(
        shards,
        mesh=mesh,
        in_specs=(
            P("ctx", "head"),
            P("ctx"),
            P(None, "head"),
            P(None, "head"),
            P(None, "head"),
            P("head", None),
        ),
        out_specs=P("ctx", "head"),
        check_vma=False,
    )
```

```python
import functools

import jax
import jax.numpy as jnp
import numpy as np
from jax import lax
from jax.experimental import pallas as pl
from jax.experimental.pallas import tpu as pltpu
from jax.sharding import PartitionSpec as P

HEAD_DIM = 128
FEAT = 16
WIN = 64
SUB = 256
WIDE = 256
PART = 32
TABLE = 1536
LEAD = 128
F32 = jnp.float32
BF16 = jnp.bfloat16
MESH = pl.DeviceIdType.MESH


def selection_tables():
    first = np.zeros((FEAT, WIDE), np.float32)
    second = np.zeros((FEAT, WIDE), np.float32)
    weight = np.zeros((WIDE,), np.float32)
    for g in range(8):
        for r in range(FEAT):
            p = g * PART + r
            first[r, p] = 1.0
            second[(r + g) % FEAT, p] = 1.0
            weight[p] = 1.0 / 32 if g == 0 else 2.0 / 32
        p = g * PART + 16
        first[g, p] = 1.0
        second[g + 8, p] = 1.0
        weight[p] = 2.0 / 32
        for n in range(2):
            first[2 * g + n, p + 1 + n] = 1.0
            weight[p + 1 + n] = 0.25
    query = np.zeros((2, 2, 4 * FEAT, WIDE), np.float32)
    key = np.zeros((2, 2, WIDE, 4 * FEAT), np.float32)
    pick = np.zeros((2, 2, 4 * FEAT, 128), np.float32)
    for head in range(2):
        at = head * 2 * FEAT
        query[head, 0, at : at + FEAT] = first * weight
        query[head, 1, at : at + FEAT] = second
        key[head, 0, :, at + FEAT : at + 2 * FEAT] = first.T
        key[head, 1, :, at + FEAT : at + 2 * FEAT] = second.T
        pick[head, 0, at : at + FEAT, :FEAT] = np.eye(FEAT)
        pick[head, 1, at + FEAT : at + 2 * FEAT, :FEAT] = np.eye(FEAT)
    table = np.zeros((TABLE, WIDE), np.float32)
    table[0:256] = query.reshape(256, WIDE)
    table[256:1280, 0 : 4 * FEAT] = key.reshape(4 * WIDE, 4 * FEAT)
    table[1280:1536, 0:128] = pick.reshape(256, 128)
    return jnp.asarray(table, BF16)


def dot(a, b):
    return lax.dot_general(a, b, (((1,), (0,)), ((), ())), preferred_element_type=F32)


def dot_nt(a, b):
    return lax.dot_general(a, b, (((1,), (1,)), ((), ())), preferred_element_type=F32)


def factor_bias(shape, dim):
    p = lax.broadcasted_iota(jnp.int32, shape, dim)
    one = jnp.where(p == 19, 1.0, 0.0)
    two = jnp.where((p == 19) | (p % PART == 17) | (p % PART == 18), 1.0, 0.0)
    return one, two


def kernel(
    nctx, nz,
    tok, doc, wf_in, wv_in, ww_in, wo_in, table_in,
    out,
    gath, wf, wv, ww, af, av, aw, table,
    feat, wq, kcat, vcat, docc, docr, fq, fk, phiq,
    docs, lin, win, st_acc, st_send, st_recv, st_sums, st, mix, wo, sbuf, rbuf,
    load_sem, tok_sem, wo_sem, ring_send, ring_recv, par_send, par_recv,
    wo_send, wo_recv, doc_send, doc_recv, st_ssem, st_rsem, sum_ssem, sum_rsem, tail_send, tail_recv,
    mix_send, mix_recv, rs_send, rs_recv,
):
    n_sub = tok.shape[0] // SUB
    assert n_sub == 4
    units = n_sub * nz
    rows_total = tok.shape[0]
    part = WIDE // nctx
    b = lax.axis_index("ctx")
    head = lax.axis_index("head")
    z = head // 2
    k = head - 2 * z
    other = 1 - k
    way = 1 - 2 * k
    ahead = lax.rem(z + way + nz, nz) * 2 + k
    behind = lax.rem(z - way + nz, nz) * 2 + k
    partner = z * 2 + other

    def sub_rows(i):
        return pl.ds(pl.multiple_of(i * SUB, SUB), SUB)

    def cols(block):
        return pl.ds(pl.multiple_of(block * 256, 256), 256)

    def bulk(ref, sem):
        return pltpu.make_async_copy(ref, ref, sem.at[0])

    loads = [
        pltpu.make_async_copy(src, dst, load_sem.at[n])
        for n, (src, dst) in enumerate(
            [(wf_in, wf), (wv_in, wv), (ww_in, ww), (table_in, table)]
        )
    ]

    def tok_load(i):
        return pltpu.make_async_copy(tok.at[sub_rows(i)], gath.at[k, z, sub_rows(i)], tok_sem.at[i])

    for i in range(n_sub):
        tok_load(i).start()
    for load in loads:
        load.start()

    kcat[0:LEAD, :] = jnp.zeros((LEAD, 256), BF16)
    vcat[0:LEAD, :] = jnp.zeros((LEAD, 256), BF16)

    barrier = pltpu.get_barrier_semaphore()

    def greet(n, carry):
        pl.semaphore_signal(
            barrier, inc=1, device_id={"ctx": lax.rem(b + 1 + n, nctx)}, device_id_type=MESH
        )
        return carry

    for peer in (ahead, behind, partner):
        pl.semaphore_signal(barrier, inc=1, device_id={"head": peer}, device_id_type=MESH)
    lax.fori_loop(0, nctx - 1, greet, 0)
    af[...] = jnp.zeros_like(af)
    av[...] = jnp.zeros_like(av)
    aw[...] = jnp.zeros_like(aw)
    pl.semaphore_wait(barrier, nctx + 2)

    def ring_copy(u):
        s = u // n_sub
        rows = sub_rows(u - s * n_sub)
        src = lax.rem(z - s * way + 2 * nz, nz)
        return pltpu.make_async_remote_copy(
            src_ref=gath.at[k, src, rows],
            dst_ref=gath.at[k, src, rows],
            send_sem=ring_send.at[0],
            recv_sem=ring_recv.at[u],
            device_id={"head": ahead},
            device_id_type=MESH,
        )

    def ring_arrival(u):
        s = u // n_sub
        rows = sub_rows(u - s * n_sub)
        src = lax.rem(z - s * way + 2 * nz, nz)
        slot = gath.at[k, src, rows]
        return pltpu.make_async_remote_copy(
            src_ref=slot,
            dst_ref=slot,
            send_sem=ring_send.at[0],
            recv_sem=ring_recv.at[u - n_sub],
            device_id={"head": ahead},
            device_id_type=MESH,
        )

    def par_copy(u, side, turn):
        s = u // n_sub
        rows = sub_rows(u - s * n_sub)
        src = lax.rem(z - s * turn + 2 * nz, nz)
        slot = gath.at[side, src, rows]
        return pltpu.make_async_remote_copy(
            src_ref=slot,
            dst_ref=slot,
            send_sem=par_send.at[0],
            recv_sem=par_recv.at[u],
            device_id={"head": partner},
            device_id_type=MESH,
        )

    def accumulate(u, side, turn):
        s = u // n_sub
        rows = sub_rows(u - s * n_sub)
        src = lax.rem(z - s * turn + 2 * nz, nz)
        x = gath[side, src, rows, :]
        w_rows = cols(src * 2 + side)
        af[rows, :] += dot_nt(x, wf[:, w_rows])
        av[rows, :] += dot(x, wv[w_rows, :])
        aw[rows, :] += dot(x, ww[w_rows, :])

    for i in range(n_sub):
        tok_load(i).wait()
        ring_copy(i).start()
        par_copy(i, k, way).start()

    def doc_copy(c, slot):
        return pltpu.make_async_remote_copy(
            src_ref=doc,
            dst_ref=docs.at[slot],
            send_sem=doc_send.at[0],
            recv_sem=doc_recv.at[0],
            device_id={"ctx": c},
            device_id_type=MESH,
        )

    def wo_copy(d, side, target):
        return pltpu.make_async_remote_copy(
            src_ref=wo_in.at[:, cols(d * 2 + target)],
            dst_ref=wo.at[side, d],
            send_sem=wo_send.at[0],
            recv_sem=wo_recv.at[0],
            device_id={"head": partner},
            device_id_type=MESH,
        )

    def wo_load(d):
        return pltpu.make_async_copy(wo_in.at[:, cols(d * 2 + k)], wo.at[k, d], wo_sem.at[0])

    def start_doc(n, carry):
        doc_copy(lax.rem(b + n, nctx), b).start()
        return carry

    lax.fori_loop(1, nctx, start_doc, 0)

    def start_wo(d, carry):
        wo_copy(d, k, other).start()
        wo_load(d).start()
        return carry

    lax.fori_loop(0, nz, start_wo, 0)

    mine = doc[...].astype(F32)
    last_doc = mine[7:8, 127:128]
    for i in range(8):
        row = mine[i : i + 1, :]
        docr[0:1, LEAD + i * 128 : LEAD + (i + 1) * 128] = row
        docc[i * 128 : (i + 1) * 128, :] = jnp.broadcast_to(row, (128, 128)).T

    st_acc[...] = jnp.zeros_like(st_acc)
    for load in loads:
        load.wait()

    lag = 6

    def own_unit(u):
        @pl.when(u >= n_sub)
        def _():
            ring_arrival(u).wait_recv()

            @pl.when(u < units - n_sub)
            def _():
                ring_copy(u).start()

            par_copy(u, k, way).start()

        accumulate(u, k, way)

    def partner_unit(u):
        par_copy(u, other, -way).wait_recv()
        accumulate(u, other, -way)

    def ring_step(u, carry):
        own_unit(u)

        @pl.when(u >= lag)
        def _():
            partner_unit(u - lag)

        return carry

    turn = units - n_sub
    lax.fori_loop(0, turn, ring_step, 0)

    one_k, two_k = factor_bias((WIDE, 1), 0)

    def finish(i):
        rows = sub_rows(i)
        late = pl.ds(pl.multiple_of(LEAD + i * SUB, 128), SUB)
        x = af[rows, :].astype(BF16)
        v = av[rows, :].astype(BF16)
        feat[rows, :] = x
        vcat[late, :] = v
        keeps = docr[0:1, late] == last_doc
        for j in range(2):
            at = 256 + 512 * j
            left = dot_nt(table[at : at + 256, 0:64], x) + one_k
            right = dot_nt(table[at + 256 : at + 512, 0:64], x) + two_k
            phi_k = jnp.where(keeps, left * right, 0.0).astype(BF16)
            st_acc[j] += dot(phi_k, v[:, j * 128 : (j + 1) * 128])
        wq[rows, 0:128] = aw[rows, 0:128].astype(BF16)
        kcat[late, 0:128] = aw[rows, 128:256].astype(BF16)
        wq[rows, 128:256] = aw[rows, 256:384].astype(BF16)
        kcat[late, 128:256] = aw[rows, 384:512].astype(BF16)

    def catch_up(n, carry):
        own_unit(turn + n)

        def partner_next(m, inner):
            partner_unit(turn - lag + 3 * n + m)
            return inner

        lax.fori_loop(0, 3, partner_next, 0)
        return carry

    def finish_early(n, carry):
        own_unit(turn + 2 + n)
        partner_unit(turn + n)
        finish(n)
        return carry

    def finish_late(n, carry):
        partner_unit(turn + 2 + n)
        finish(2 + n)
        return carry

    lax.fori_loop(0, 2, catch_up, 0)
    lax.fori_loop(0, 2, finish_early, 0)
    lax.fori_loop(0, 2, finish_late, 0)

    def tail_copy(n):
        buf = (kcat, vcat)[n]
        return pltpu.make_async_remote_copy(
            src_ref=buf.at[LEAD + rows_total - WIN : LEAD + rows_total],
            dst_ref=buf.at[LEAD - WIN : LEAD],
            send_sem=tail_send.at[n],
            recv_sem=tail_recv.at[n],
            device_id={"ctx": lax.rem(b + 1, nctx)},
            device_id_type=MESH,
        )

    for j in range(2):
        st_send[:, j * part : (j + 1) * part, :] = st_acc[j].astype(BF16).reshape(nctx, part, 128)

    def st_copy(c, slot):
        return pltpu.make_async_remote_copy(
            src_ref=st_send.at[c],
            dst_ref=st_recv.at[slot],
            send_sem=st_ssem.at[0],
            recv_sem=st_rsem.at[0],
            device_id={"ctx": c},
            device_id_type=MESH,
        )

    def start_state(n, carry):
        st_copy(lax.rem(b + n, nctx), b).start()
        return carry

    lax.fori_loop(1, nctx, start_state, 0)

    @pl.when(b < nctx - 1)
    def _():
        tail_copy(0).start()
        tail_copy(1).start()

    one_q, two_q = factor_bias((1, WIDE), 1)

    def query_rows(i, carry):
        rows = sub_rows(i)
        x = feat[rows, :]
        for j in range(2):
            left = dot(x, table[128 * j : 128 * j + 64, :]) + one_q
            right = dot(x, table[128 * j + 64 : 128 * j + 128, :]) + two_q
            phiq[j, rows, :] = (left * right).astype(BF16)
            at = 1280 + 128 * j
            fq[j, rows, :] = dot(x, table[at : at + 64, 0:128]).astype(BF16)
            fk[j, rows, :] = dot(x, table[at + 64 : at + 128, 0:128]).astype(BF16)
        return carry

    lax.fori_loop(0, n_sub, query_rows, 0)

    for i in range(n_sub):
        lo, hi = i * SUB, (i + 1) * SUB
        t_pos = lax.broadcasted_iota(jnp.int32, (SUB, hi), 0) + lo
        s_pos = lax.broadcasted_iota(jnp.int32, (SUB, hi), 1)
        allowed = (s_pos <= t_pos) & (docc[lo:hi, 0:1] == docr[0:1, LEAD : LEAD + hi])
        for j in range(2):
            d = dot_nt(fq[j, lo:hi, :], fk[j, 0:hi, :])
            taylor = jnp.where(allowed, 1.0 + d * (0.25 + d * 0.03125), 0.0).astype(BF16)
            lin[lo:hi, j * 128 : (j + 1) * 128] = dot(
                taylor, vcat[LEAD : LEAD + hi, j * 128 : (j + 1) * 128]
            )

    def sum_back(c, slot):
        return pltpu.make_async_remote_copy(
            src_ref=st_sums.at[c],
            dst_ref=st.at[slot],
            send_sem=sum_ssem.at[0],
            recv_sem=sum_rsem.at[0],
            device_id={"ctx": c},
            device_id_type=MESH,
        )

    bulk(docs.at[0 : nctx - 1], doc_recv).wait()
    bulk(st_recv.at[0 : nctx - 1], st_rsem).wait()
    docs[b] = doc[...]
    st_recv[b] = st_send[b]

    sums = jnp.zeros((2 * part, 128), F32)
    for c in range(nctx - 1):
        same = docs[c][7:8, 127:128] == docs[max(c - 1, 0)][7:8, 127:128]
        sums = st_recv[c].astype(F32) + jnp.where(same, sums, 0.0)
        st_sums[c + 1] = sums.astype(BF16)

    def start_sum(n, carry):
        c = lax.rem(b + n, nctx)

        @pl.when(c > 0)
        def _():
            sum_back(c, b).start()

        return carry

    lax.fori_loop(1, nctx, start_sum, 0)

    @pl.when(b == 0)
    def _():
        docr[0:1, 0:LEAD] = jnp.full((1, LEAD), -1.0, F32)

    @pl.when(b > 0)
    def _():
        tail_copy(0).wait_recv()
        tail_copy(1).wait_recv()
        docr[0:1, 0:LEAD] = docs[b - 1][7:8, :].astype(F32)

    reach = LEAD + SUB
    gap = lax.broadcasted_iota(jnp.int32, (SUB, reach), 1) - lax.broadcasted_iota(
        jnp.int32, (SUB, reach), 0
    )
    band = (gap > LEAD - WIN) & (gap <= LEAD)
    for i in range(n_sub):
        lo, hi = i * SUB, (i + 1) * SUB
        within = band & (docc[lo:hi, 0:1] == docr[0:1, lo : lo + reach])
        for j in range(2):
            at = slice(j * 128, (j + 1) * 128)
            logits = dot_nt(wq[lo:hi, at], kcat[lo : lo + reach, at]) * HEAD_DIM ** (-0.5)
            logits = jnp.where(within, logits, -1e30)
            top = jnp.max(logits, -1, keepdims=True)
            weights = jnp.where(within, jnp.exp(logits - top), 0.0)
            probs = (weights / jnp.sum(weights, -1, keepdims=True)).astype(BF16)
            win[lo:hi, at] = dot(probs, vcat[lo : lo + reach, at])

    @pl.when(b == 0)
    def _():
        st[...] = jnp.zeros_like(st)

    @pl.when(b > 0)
    def _():
        bulk(st.at[0 : nctx - 1], sum_rsem).wait()
        st[b] = st_sums[b]

    state = [
        st[:, j * part : (j + 1) * part, :].reshape(WIDE, 128) for j in range(2)
    ]

    def mix_copy(i, side):
        slot = mix.at[side, sub_rows(i)]
        return pltpu.make_async_remote_copy(
            src_ref=slot,
            dst_ref=slot,
            send_sem=mix_send.at[0],
            recv_sem=mix_recv.at[i],
            device_id={"head": partner},
            device_id_type=MESH,
        )

    def mix_rows(i, carry):
        rows = sub_rows(i)
        uses = docc[rows, :] == docr[0:1, LEAD - 1 : LEAD]
        for j in range(2):
            at = slice(j * 128, (j + 1) * 128)
            carried = dot(phiq[j, rows, :], state[j])
            linear = lin[rows, at] + jnp.where(uses, carried, 0.0)
            square = jnp.mean(linear * linear, -1, keepdims=True)
            normed = linear * lax.rsqrt(square + 1e-5)
            mix[k, rows, at] = (normed + win[rows, at]).astype(BF16)
        mix_copy(i, k).start()
        return carry


    bulk(wo.at[k], wo_sem).wait()
    bulk(wo.at[other], wo_recv).wait()

    def sum_copy(u):
        s = u // n_sub
        i = u - s * n_sub
        return pltpu.make_async_remote_copy(
            src_ref=sbuf.at[s, i],
            dst_ref=rbuf.at[s, i],
            send_sem=rs_send.at[0],
            recv_sem=rs_recv.at[u],
            device_id={"head": ahead},
            device_id_type=MESH,
        )

    def sum_step(u, carry):
        s = u // n_sub
        i = u - s * n_sub
        rows = sub_rows(i)
        dest = lax.rem(z - (s + 1) * way + 2 * nz, nz)

        @pl.when(u < n_sub)
        def _():
            mix_copy(i, other).wait_recv()

        part = dot(mix[0, rows, :], wo[0, dest]) + dot(mix[1, rows, :], wo[1, dest])

        @pl.when(u < n_sub)
        def _():
            sbuf[s, i] = part.astype(BF16)
            sum_copy(u).start()

        @pl.when(u >= n_sub)
        def _():
            sum_copy(u - n_sub).wait_recv()
            both = (part + rbuf[s - 1, i].astype(F32)).astype(BF16)

            @pl.when(u < units - n_sub)
            def _():
                sbuf[s, i] = both
                sum_copy(u).start()

            @pl.when(u >= units - n_sub)
            def _():
                out[rows, :] = both

        return carry

    def first_step(i, carry):
        @pl.when(i < n_sub)
        def _():
            mix_rows(i, 0)

        @pl.when(i > 0)
        def _():
            sum_step(i - 1, 0)

        return carry

    lax.fori_loop(0, n_sub + 1, first_step, 0)
    lax.fori_loop(n_sub, units, sum_step, 0)

    bulk(gath.at[k, 0 : nz - 1], ring_send).wait()
    bulk(gath.at[k], par_send).wait()
    bulk(sbuf, rs_send).wait()
    bulk(docs.at[0 : nctx - 1], doc_send).wait()
    bulk(st_send.at[0 : nctx - 1], st_ssem).wait()
    bulk(mix.at[k], mix_send).wait()
    bulk(wo.at[k], wo_send).wait()

    @pl.when(b == 0)
    def _():
        bulk(st_sums.at[0 : nctx - 1], sum_ssem).wait()

    @pl.when(b > 0)
    def _():
        bulk(st_sums.at[0 : nctx - 2], sum_ssem).wait()

    @pl.when(b < nctx - 1)
    def _():
        tail_copy(0).wait_send()
        tail_copy(1).wait_send()


def solution(mesh):
    nctx, nhead = mesh.shape["ctx"], mesh.shape["head"]
    nz = nhead // 2

    def shards(tokens, doc_ids, w_feat, w_value, w_window, w_out):
        rows = tokens.shape[0]
        width = w_value.shape[0]
        n_sub = rows // SUB
        units = n_sub * nz
        dma = pltpu.SemaphoreType.DMA
        vmem = pltpu.VMEM
        hbm_space = pl.BlockSpec(memory_space=pltpu.HBM)
        vmem_space = pl.BlockSpec(memory_space=pltpu.VMEM)
        return pl.pallas_call(
            functools.partial(kernel, nctx, nz),
            out_shape=jax.ShapeDtypeStruct((rows, 256), BF16),
            in_specs=[hbm_space, vmem_space] + [hbm_space] * 5,
            out_specs=vmem_space,
            scratch_shapes=[
                vmem((2, nz, rows, 256), BF16),
                vmem((64, width), BF16),
                vmem((width, 256), BF16),
                vmem((width, 512), BF16),
                vmem((rows, 64), F32),
                vmem((rows, 256), F32),
                vmem((rows, 512), F32),
                vmem((TABLE, WIDE), BF16),
                vmem((rows, 64), BF16),
                vmem((rows, 256), BF16),
                vmem((LEAD + rows, 256), BF16),
                vmem((LEAD + rows, 256), BF16),
                vmem((rows, 128), F32),
                vmem((1, LEAD + rows), F32),
                vmem((2, rows, 128), BF16),
                vmem((2, rows, 128), BF16),
                vmem((2, rows, WIDE), BF16),
                vmem((nctx, 8, 128), jnp.int32),
                vmem((rows, 256), F32),
                vmem((rows, 256), F32),
                vmem((2, WIDE, 128), F32),
                vmem((nctx, 2 * WIDE // nctx, 128), BF16),
                vmem((nctx, 2 * WIDE // nctx, 128), BF16),
                vmem((nctx, 2 * WIDE // nctx, 128), BF16),
                vmem((nctx, 2 * WIDE // nctx, 128), BF16),
                vmem((2, rows, 256), BF16),
                vmem((2, nz, 256, 256), BF16),
                vmem((nz - 1, n_sub, SUB, 256), BF16),
                vmem((nz - 1, n_sub, SUB, 256), BF16),
                dma((4,)),
                dma((n_sub,)),
                dma((1,)),
                dma((1,)),
                dma((units,)),
                dma((1,)),
                dma((units,)),
                dma((1,)),
                dma((1,)),
                dma((1,)),
                dma((1,)),
                dma((1,)),
                dma((1,)),
                dma((1,)),
                dma((1,)),
                dma((2,)),
                dma((2,)),
                dma((1,)),
                dma((n_sub,)),
                dma((1,)),
                dma((units,)),
            ],
            compiler_params=pltpu.CompilerParams(
                collective_id=0, has_side_effects=True, vmem_limit_bytes=67043328 - 11000 * 1024
            ),
            name="based_layer",
        )(
            tokens,
            doc_ids.reshape(8, 128),
            w_feat.T,
            w_value,
            w_window,
            w_out,
            selection_tables(),
        )

    return jax.shard_map(
        shards,
        mesh=mesh,
        in_specs=(
            P("ctx", "head"),
            P("ctx"),
            P(None, "head"),
            P(None, "head"),
            P(None, "head"),
            P("head", None),
        ),
        out_specs=P("ctx", "head"),
        check_vma=False,
    )
```

```python
import functools

import jax
import jax.numpy as jnp
import numpy as np
from jax import lax
from jax.experimental import pallas as pl
from jax.experimental.pallas import tpu as pltpu
from jax.sharding import PartitionSpec as P

HEAD_DIM = 128
FEAT = 16
WIN = 64
SUB = 256
WIDE = 256
PART = 32
TABLE = 1536
LEAD = 128
F32 = jnp.float32
BF16 = jnp.bfloat16
MESH = pl.DeviceIdType.MESH


def selection_tables():
    first = np.zeros((FEAT, WIDE), np.float32)
    second = np.zeros((FEAT, WIDE), np.float32)
    weight = np.zeros((WIDE,), np.float32)
    for g in range(8):
        for r in range(FEAT):
            p = g * PART + r
            first[r, p] = 1.0
            second[(r + g) % FEAT, p] = 1.0
            weight[p] = 1.0 / 32 if g == 0 else 2.0 / 32
        p = g * PART + 16
        first[g, p] = 1.0
        second[g + 8, p] = 1.0
        weight[p] = 2.0 / 32
        for n in range(2):
            first[2 * g + n, p + 1 + n] = 1.0
            weight[p + 1 + n] = 0.25
    query = np.zeros((2, 2, 4 * FEAT, WIDE), np.float32)
    key = np.zeros((2, 2, WIDE, 4 * FEAT), np.float32)
    pick = np.zeros((2, 2, 4 * FEAT, 128), np.float32)
    for head in range(2):
        at = head * 2 * FEAT
        query[head, 0, at : at + FEAT] = first * weight
        query[head, 1, at : at + FEAT] = second
        key[head, 0, :, at + FEAT : at + 2 * FEAT] = first.T
        key[head, 1, :, at + FEAT : at + 2 * FEAT] = second.T
        pick[head, 0, at : at + FEAT, :FEAT] = np.eye(FEAT)
        pick[head, 1, at + FEAT : at + 2 * FEAT, :FEAT] = np.eye(FEAT)
    table = np.zeros((TABLE, WIDE), np.float32)
    table[0:256] = query.reshape(256, WIDE)
    table[256:1280, 0 : 4 * FEAT] = key.reshape(4 * WIDE, 4 * FEAT)
    table[1280:1536, 0:128] = pick.reshape(256, 128)
    return jnp.asarray(table, BF16)


def dot(a, b):
    return lax.dot_general(a, b, (((1,), (0,)), ((), ())), preferred_element_type=F32)


def dot_nt(a, b):
    return lax.dot_general(a, b, (((1,), (1,)), ((), ())), preferred_element_type=F32)


def factor_bias(shape, dim):
    p = lax.broadcasted_iota(jnp.int32, shape, dim)
    one = jnp.where(p == 19, 1.0, 0.0)
    two = jnp.where((p == 19) | (p % PART == 17) | (p % PART == 18), 1.0, 0.0)
    return one, two


def kernel(
    nctx, nz,
    tok, doc_in, wf_in, wv_in, ww_in, wo_in, table_in,
    out,
    doc, gath, wf, wv, ww, af, av, aw, table,
    feat, wq, kcat, vcat, docc, docr, fq, fk, phiq,
    docs, lin, win, st_acc, st_send, st_recv, st_sums, st, mix, wo, sbuf, rbuf,
    load_sem, tok_sem, wo_sem, ring_send, ring_recv, par_send, par_recv,
    wo_send, wo_recv, doc_send, doc_recv, st_ssem, st_rsem, sum_ssem, sum_rsem, tail_send, tail_recv,
    mix_send, mix_recv, rs_send, rs_recv,
):
    n_sub = tok.shape[0] // SUB
    assert n_sub == 4
    units = n_sub * nz
    rows_total = tok.shape[0]
    part = WIDE // nctx
    b = lax.axis_index("ctx")
    head = lax.axis_index("head")
    z = head // 2
    k = head - 2 * z
    other = 1 - k
    way = 1 - 2 * k
    ahead = lax.rem(z + way + nz, nz) * 2 + k
    behind = lax.rem(z - way + nz, nz) * 2 + k
    partner = z * 2 + other

    far_first = sorted(range(1, nctx), key=lambda n: -min(n // 4, 4 - n // 4) - min(n % 4, 4 - n % 4))

    def sub_rows(i):
        return pl.ds(pl.multiple_of(i * SUB, SUB), SUB)

    def cols(block):
        return pl.ds(pl.multiple_of(block * 256, 256), 256)

    barrier = pltpu.get_barrier_semaphore()

    def greet(n, carry):
        pl.semaphore_signal(
            barrier, inc=1, device_id={"ctx": lax.rem(b + 1 + n, nctx)}, device_id_type=MESH
        )
        return carry

    for peer in (ahead, behind, partner):
        pl.semaphore_signal(barrier, inc=1, device_id={"head": peer}, device_id_type=MESH)
    lax.fori_loop(0, nctx - 1, greet, 0)

    def bulk(ref, sem):
        return pltpu.make_async_copy(ref, ref, sem.at[0])

    loads = [
        pltpu.make_async_copy(src, dst, load_sem.at[n])
        for n, (src, dst) in enumerate(
            [(doc_in, doc), (wf_in, wf), (wv_in, wv), (ww_in, ww), (table_in, table)]
        )
    ]

    def tok_load(i):
        return pltpu.make_async_copy(tok.at[sub_rows(i)], gath.at[k, z, sub_rows(i)], tok_sem.at[i])

    for i in range(n_sub):
        tok_load(i).start()
    for load in loads:
        load.start()

    af[...] = jnp.zeros_like(af)
    av[...] = jnp.zeros_like(av)
    aw[...] = jnp.zeros_like(aw)
    st_acc[...] = jnp.zeros_like(st_acc)
    no_rows = jnp.zeros((LEAD - WIN, 256), BF16)
    for buf in (kcat, vcat):
        buf[0 : LEAD - WIN, :] = no_rows

    @pl.when(b == 0)
    def _():
        for buf in (kcat, vcat):
            buf[LEAD - WIN : LEAD, :] = no_rows

    pl.semaphore_wait(barrier, nctx + 2)

    def ring_copy(u):
        s = u // n_sub
        rows = sub_rows(u - s * n_sub)
        src = lax.rem(z - s * way + 2 * nz, nz)
        return pltpu.make_async_remote_copy(
            src_ref=gath.at[k, src, rows],
            dst_ref=gath.at[k, src, rows],
            send_sem=ring_send.at[0],
            recv_sem=ring_recv.at[u],
            device_id={"head": ahead},
            device_id_type=MESH,
        )

    def ring_arrival(u):
        s = u // n_sub
        rows = sub_rows(u - s * n_sub)
        src = lax.rem(z - s * way + 2 * nz, nz)
        slot = gath.at[k, src, rows]
        return pltpu.make_async_remote_copy(
            src_ref=slot,
            dst_ref=slot,
            send_sem=ring_send.at[0],
            recv_sem=ring_recv.at[u - n_sub],
            device_id={"head": ahead},
            device_id_type=MESH,
        )

    def par_copy(u, side, turn):
        s = u // n_sub
        rows = sub_rows(u - s * n_sub)
        src = lax.rem(z - s * turn + 2 * nz, nz)
        slot = gath.at[side, src, rows]
        return pltpu.make_async_remote_copy(
            src_ref=slot,
            dst_ref=slot,
            send_sem=par_send.at[0],
            recv_sem=par_recv.at[u],
            device_id={"head": partner},
            device_id_type=MESH,
        )

    def accumulate(u, side, turn, what="both"):
        s = u // n_sub
        rows = sub_rows(u - s * n_sub)
        src = lax.rem(z - s * turn + 2 * nz, nz)
        x = gath[side, src, rows, :]
        w_rows = cols(src * 2 + side)
        if what != "window":
            af[rows, :] += dot_nt(x, wf[:, w_rows])
            av[rows, :] += dot(x, wv[w_rows, :])
        if what != "state":
            aw[rows, :] += dot(x, ww[w_rows, :])

    for i in range(n_sub):
        tok_load(i).wait()
        ring_copy(i).start()
        par_copy(i, k, way).start()

    loads[0].wait()

    def doc_copy(c, slot):
        return pltpu.make_async_remote_copy(
            src_ref=doc,
            dst_ref=docs.at[slot],
            send_sem=doc_send.at[0],
            recv_sem=doc_recv.at[0],
            device_id={"ctx": c},
            device_id_type=MESH,
        )

    def wo_copy(d, side, target):
        return pltpu.make_async_remote_copy(
            src_ref=wo_in.at[:, cols(d * 2 + target)],
            dst_ref=wo.at[side, d],
            send_sem=wo_send.at[0],
            recv_sem=wo_recv.at[0],
            device_id={"head": partner},
            device_id_type=MESH,
        )

    def wo_load(d):
        return pltpu.make_async_copy(wo_in.at[:, cols(d * 2 + k)], wo.at[k, d], wo_sem.at[0])

    def start_doc(n, carry):
        doc_copy(lax.rem(b + n, nctx), b).start()
        return carry

    lax.fori_loop(1, nctx, start_doc, 0)

    def start_wo(d, carry):
        wo_copy(d, k, other).start()
        wo_load(d).start()
        return carry

    lax.fori_loop(0, nz, start_wo, 0)

    mine = doc[...].astype(F32)
    last_doc = mine[7:8, 127:128]
    for i in range(8):
        row = mine[i : i + 1, :]
        docr[0:1, LEAD + i * 128 : LEAD + (i + 1) * 128] = row
        docc[i * 128 : (i + 1) * 128, :] = jnp.broadcast_to(row, (128, 128)).T

    for load in loads[1:]:
        load.wait()

    lag = 6

    def own_unit(u):
        @pl.when(u >= n_sub)
        def _():
            ring_arrival(u).wait_recv()

            @pl.when(u < units - n_sub)
            def _():
                ring_copy(u).start()

            par_copy(u, k, way).start()

        accumulate(u, k, way)

    def partner_unit(u, what="both"):
        par_copy(u, other, -way).wait_recv()
        accumulate(u, other, -way, what)

    def ring_step(u, carry):
        own_unit(u)

        @pl.when(u >= lag)
        def _():
            partner_unit(u - lag)

        return carry

    turn = units - n_sub
    lax.fori_loop(0, turn, ring_step, 0)

    one_k, two_k = factor_bias((WIDE, 1), 0)

    def finish(i):
        rows = sub_rows(i)
        late = pl.ds(pl.multiple_of(LEAD + i * SUB, 128), SUB)
        x = af[rows, :].astype(BF16)
        v = av[rows, :].astype(BF16)
        feat[rows, :] = x
        vcat[late, :] = v
        keeps = docr[0:1, late] == last_doc
        for j in range(2):
            at = 256 + 512 * j
            left = dot_nt(table[at : at + 256, 0:64], x) + one_k
            right = dot_nt(table[at + 256 : at + 512, 0:64], x) + two_k
            phi_k = jnp.where(keeps, left * right, 0.0).astype(BF16)
            st_acc[j] += dot(phi_k, v[:, j * 128 : (j + 1) * 128])

    def catch_up(n, carry):
        own_unit(turn + n)

        def partner_next(m, inner):
            partner_unit(turn - lag + 3 * n + m)
            return inner

        lax.fori_loop(0, 3, partner_next, 0)
        return carry

    def finish_early(n, carry):
        own_unit(turn + 2 + n)
        partner_unit(turn + n)
        finish(n)
        return carry

    def finish_late(n, carry):
        partner_unit(turn + 2 + n, "state")
        finish(2 + n)
        return carry

    lax.fori_loop(0, 2, catch_up, 0)
    lax.fori_loop(0, 2, finish_early, 0)
    lax.fori_loop(0, 2, finish_late, 0)

    def tail_copy(n):
        buf = (kcat, vcat)[n]
        return pltpu.make_async_remote_copy(
            src_ref=buf.at[LEAD + rows_total - WIN : LEAD + rows_total],
            dst_ref=buf.at[LEAD - WIN : LEAD],
            send_sem=tail_send.at[n],
            recv_sem=tail_recv.at[n],
            device_id={"ctx": lax.rem(b + 1, nctx)},
            device_id_type=MESH,
        )

    for j in range(2):
        st_send[:, j * part : (j + 1) * part, :] = st_acc[j].astype(BF16).reshape(nctx, part, 128)

    def st_copy(c, slot):
        return pltpu.make_async_remote_copy(
            src_ref=st_send.at[c],
            dst_ref=st_recv.at[slot],
            send_sem=st_ssem.at[0],
            recv_sem=st_rsem.at[0],
            device_id={"ctx": c},
            device_id_type=MESH,
        )

    for n in far_first:
        st_copy(lax.rem(b + n, nctx), b).start()

    def window_rows(i, carry):
        rows = sub_rows(i)
        late = pl.ds(pl.multiple_of(LEAD + i * SUB, 128), SUB)
        wq[rows, 0:128] = aw[rows, 0:128].astype(BF16)
        kcat[late, 0:128] = aw[rows, 128:256].astype(BF16)
        wq[rows, 128:256] = aw[rows, 256:384].astype(BF16)
        kcat[late, 128:256] = aw[rows, 384:512].astype(BF16)
        return carry

    def window_late(n, carry):
        accumulate(turn + 2 + n, other, -way, "window")
        return carry

    lax.fori_loop(0, 2, window_late, 0)
    lax.fori_loop(0, n_sub, window_rows, 0)

    @pl.when(b < nctx - 1)
    def _():
        tail_copy(0).start()
        tail_copy(1).start()

    one_q, two_q = factor_bias((1, WIDE), 1)

    def query_rows(i, carry):
        rows = sub_rows(i)
        x = feat[rows, :]
        for j in range(2):
            left = dot(x, table[128 * j : 128 * j + 64, :]) + one_q
            right = dot(x, table[128 * j + 64 : 128 * j + 128, :]) + two_q
            phiq[j, rows, :] = (left * right).astype(BF16)
            at = 1280 + 128 * j
            fq[j, rows, :] = dot(x, table[at : at + 64, 0:128]).astype(BF16)
            fk[j, rows, :] = dot(x, table[at + 64 : at + 128, 0:128]).astype(BF16)
        return carry

    lax.fori_loop(0, n_sub, query_rows, 0)

    for i in range(n_sub):
        lo, hi = i * SUB, (i + 1) * SUB
        t_pos = lax.broadcasted_iota(jnp.int32, (SUB, hi), 0) + lo
        s_pos = lax.broadcasted_iota(jnp.int32, (SUB, hi), 1)
        allowed = (s_pos <= t_pos) & (docc[lo:hi, 0:1] == docr[0:1, LEAD : LEAD + hi])
        for j in range(2):
            d = dot_nt(fq[j, lo:hi, :], fk[j, 0:hi, :])
            taylor = jnp.where(allowed, 1.0 + d * (0.25 + d * 0.03125), 0.0).astype(BF16)
            lin[lo:hi, j * 128 : (j + 1) * 128] = dot(
                taylor, vcat[LEAD : LEAD + hi, j * 128 : (j + 1) * 128]
            )

    def sum_back(c, slot):
        return pltpu.make_async_remote_copy(
            src_ref=st_sums.at[c],
            dst_ref=st.at[slot],
            send_sem=sum_ssem.at[0],
            recv_sem=sum_rsem.at[0],
            device_id={"ctx": c},
            device_id_type=MESH,
        )

    bulk(docs.at[0 : nctx - 1], doc_recv).wait()
    bulk(st_recv.at[0 : nctx - 1], st_rsem).wait()
    docs[b] = doc[...]
    st_recv[b] = st_send[b]

    sums = jnp.zeros((2 * part, 128), F32)
    for c in range(nctx - 1):
        same = docs[c][7:8, 127:128] == docs[max(c - 1, 0)][7:8, 127:128]
        sums = st_recv[c].astype(F32) + jnp.where(same, sums, 0.0)
        st_sums[c + 1] = sums.astype(BF16)

    def start_sum(c):
        @pl.when(c > 0)
        def _():
            sum_back(c, b).start()

    for n in far_first:
        start_sum(lax.rem(b + n, nctx))

    @pl.when(b == 0)
    def _():
        docr[0:1, 0:LEAD] = jnp.full((1, LEAD), -1.0, F32)

    @pl.when(b > 0)
    def _():
        tail_copy(0).wait_recv()
        tail_copy(1).wait_recv()
        docr[0:1, 0:LEAD] = docs[b - 1][7:8, :].astype(F32)

    tile, reach = 128, LEAD + 128
    gap = lax.broadcasted_iota(jnp.int32, (tile, reach), 1) - lax.broadcasted_iota(
        jnp.int32, (tile, reach), 0
    )
    band = (gap > LEAD - WIN) & (gap <= LEAD)
    for i in range(rows_total // tile):
        lo, hi = i * tile, (i + 1) * tile
        within = band & (docc[lo:hi, 0:1] == docr[0:1, lo : lo + reach])
        for j in range(2):
            at = slice(j * 128, (j + 1) * 128)
            logits = jnp.where(within, dot_nt(wq[lo:hi, at], kcat[lo : lo + reach, at]), -1e30)
            top = jnp.max(logits, -1, keepdims=True)
            weights = jnp.exp((logits - top) * HEAD_DIM ** (-0.5))
            probs = (weights * (1.0 / jnp.sum(weights, -1, keepdims=True))).astype(BF16)
            win[lo:hi, at] = dot(probs, vcat[lo : lo + reach, at])

    @pl.when(b == 0)
    def _():
        st[...] = jnp.zeros_like(st)

    @pl.when(b > 0)
    def _():
        bulk(st.at[0 : nctx - 1], sum_rsem).wait()
        st[b] = st_sums[b]

    state = [
        st[:, j * part : (j + 1) * part, :].reshape(WIDE, 128) for j in range(2)
    ]

    def mix_copy(i, side):
        slot = mix.at[side, sub_rows(i)]
        return pltpu.make_async_remote_copy(
            src_ref=slot,
            dst_ref=slot,
            send_sem=mix_send.at[0],
            recv_sem=mix_recv.at[i],
            device_id={"head": partner},
            device_id_type=MESH,
        )

    def mix_rows(i, carry):
        rows = sub_rows(i)
        uses = docc[rows, :] == docr[0:1, LEAD - 1 : LEAD]
        for j in range(2):
            at = slice(j * 128, (j + 1) * 128)
            carried = dot(phiq[j, rows, :], state[j])
            linear = lin[rows, at] + jnp.where(uses, carried, 0.0)
            square = jnp.mean(linear * linear, -1, keepdims=True)
            normed = linear * lax.rsqrt(square + 1e-5)
            mix[k, rows, at] = (normed + win[rows, at]).astype(BF16)
        mix_copy(i, k).start()
        return carry


    bulk(wo.at[k], wo_sem).wait()
    bulk(wo.at[other], wo_recv).wait()

    def sum_copy(u):
        s = u // n_sub
        i = u - s * n_sub
        return pltpu.make_async_remote_copy(
            src_ref=sbuf.at[s, i],
            dst_ref=rbuf.at[s, i],
            send_sem=rs_send.at[0],
            recv_sem=rs_recv.at[u],
            device_id={"head": ahead},
            device_id_type=MESH,
        )

    def sum_step(u, carry):
        s = u // n_sub
        i = u - s * n_sub
        rows = sub_rows(i)
        dest = lax.rem(z - (s + 1) * way + 2 * nz, nz)

        @pl.when(u < n_sub)
        def _():
            mix_copy(i, other).wait_recv()

        part = dot(mix[0, rows, :], wo[0, dest]) + dot(mix[1, rows, :], wo[1, dest])

        @pl.when(u < n_sub)
        def _():
            sbuf[s, i] = part.astype(BF16)
            sum_copy(u).start()

        @pl.when(u >= n_sub)
        def _():
            sum_copy(u - n_sub).wait_recv()
            both = (part + rbuf[s - 1, i].astype(F32)).astype(BF16)

            @pl.when(u < units - n_sub)
            def _():
                sbuf[s, i] = both
                sum_copy(u).start()

            @pl.when(u >= units - n_sub)
            def _():
                out[rows, :] = both

        return carry

    def first_step(i, carry):
        @pl.when(i < n_sub)
        def _():
            mix_rows(i, 0)

        @pl.when(i > 0)
        def _():
            sum_step(i - 1, 0)

        return carry

    lax.fori_loop(0, n_sub + 1, first_step, 0)
    lax.fori_loop(n_sub, units, sum_step, 0)

    bulk(gath.at[k, 0 : nz - 1], ring_send).wait()
    bulk(gath.at[k], par_send).wait()
    bulk(sbuf, rs_send).wait()
    bulk(docs.at[0 : nctx - 1], doc_send).wait()
    bulk(st_send.at[0 : nctx - 1], st_ssem).wait()
    bulk(mix.at[k], mix_send).wait()
    bulk(wo.at[k], wo_send).wait()

    @pl.when(b == 0)
    def _():
        bulk(st_sums.at[0 : nctx - 1], sum_ssem).wait()

    @pl.when(b > 0)
    def _():
        bulk(st_sums.at[0 : nctx - 2], sum_ssem).wait()

    @pl.when(b < nctx - 1)
    def _():
        tail_copy(0).wait_send()
        tail_copy(1).wait_send()


def solution(mesh):
    nctx, nhead = mesh.shape["ctx"], mesh.shape["head"]
    nz = nhead // 2

    def shards(tokens, doc_ids, w_feat, w_value, w_window, w_out):
        rows = tokens.shape[0]
        width = w_value.shape[0]
        n_sub = rows // SUB
        units = n_sub * nz
        dma = pltpu.SemaphoreType.DMA
        vmem = pltpu.VMEM
        hbm_space = pl.BlockSpec(memory_space=pltpu.HBM)
        vmem_space = pl.BlockSpec(memory_space=pltpu.VMEM)
        return pl.pallas_call(
            functools.partial(kernel, nctx, nz),
            out_shape=jax.ShapeDtypeStruct((rows, 256), BF16),
            in_specs=[hbm_space] * 7,
            out_specs=vmem_space,
            scratch_shapes=[
                vmem((8, 128), jnp.int32),
                vmem((2, nz, rows, 256), BF16),
                vmem((64, width), BF16),
                vmem((width, 256), BF16),
                vmem((width, 512), BF16),
                vmem((rows, 64), F32),
                vmem((rows, 256), F32),
                vmem((rows, 512), F32),
                vmem((TABLE, WIDE), BF16),
                vmem((rows, 64), BF16),
                vmem((rows, 256), BF16),
                vmem((LEAD + rows, 256), BF16),
                vmem((LEAD + rows, 256), BF16),
                vmem((rows, 128), F32),
                vmem((1, LEAD + rows), F32),
                vmem((2, rows, 128), BF16),
                vmem((2, rows, 128), BF16),
                vmem((2, rows, WIDE), BF16),
                vmem((nctx, 8, 128), jnp.int32),
                vmem((rows, 256), F32),
                vmem((rows, 256), F32),
                vmem((2, WIDE, 128), F32),
                vmem((nctx, 2 * WIDE // nctx, 128), BF16),
                vmem((nctx, 2 * WIDE // nctx, 128), BF16),
                vmem((nctx, 2 * WIDE // nctx, 128), BF16),
                vmem((nctx, 2 * WIDE // nctx, 128), BF16),
                vmem((2, rows, 256), BF16),
                vmem((2, nz, 256, 256), BF16),
                vmem((nz - 1, n_sub, SUB, 256), BF16),
                vmem((nz - 1, n_sub, SUB, 256), BF16),
                dma((5,)),
                dma((n_sub,)),
                dma((1,)),
                dma((1,)),
                dma((units,)),
                dma((1,)),
                dma((units,)),
                dma((1,)),
                dma((1,)),
                dma((1,)),
                dma((1,)),
                dma((1,)),
                dma((1,)),
                dma((1,)),
                dma((1,)),
                dma((2,)),
                dma((2,)),
                dma((1,)),
                dma((n_sub,)),
                dma((1,)),
                dma((units - n_sub,)),
            ],
            compiler_params=pltpu.CompilerParams(
                collective_id=0, has_side_effects=True, vmem_limit_bytes=67043328 - 11000 * 1024
            ),
            name="based_layer",
        )(
            tokens,
            pltpu.with_memory_space_constraint(doc_ids.reshape(8, 128), pltpu.HBM),
            w_feat.T,
            w_value,
            w_window,
            w_out,
            selection_tables(),
        )

    return jax.shard_map(
        shards,
        mesh=mesh,
        in_specs=(
            P("ctx", "head"),
            P("ctx"),
            P(None, "head"),
            P(None, "head"),
            P(None, "head"),
            P("head", None),
        ),
        out_specs=P("ctx", "head"),
        check_vma=False,
    )
```

```python
import functools

import jax
import jax.numpy as jnp
import numpy as np
from jax import lax
from jax.experimental import pallas as pl
from jax.experimental.pallas import tpu as pltpu
from jax.sharding import PartitionSpec as P

HEAD_DIM = 128
FEAT = 16
WIN = 64
SUB = 256
WIDE = 256
PART = 32
TABLE = 1408
LEAD = 128
F32 = jnp.float32
BF16 = jnp.bfloat16
MESH = pl.DeviceIdType.MESH


def selection_tables():
    first = np.zeros((FEAT, WIDE), np.float32)
    second = np.zeros((FEAT, WIDE), np.float32)
    weight = np.zeros((WIDE,), np.float32)
    for g in range(8):
        for r in range(FEAT):
            p = g * PART + r
            first[r, p] = 1.0
            second[(r + g) % FEAT, p] = 1.0
            weight[p] = 1.0 / 32 if g == 0 else 2.0 / 32
        p = g * PART + 16
        first[g, p] = 1.0
        second[g + 8, p] = 1.0
        weight[p] = 2.0 / 32
        for n in range(2):
            first[2 * g + n, p + 1 + n] = 1.0
            weight[p + 1 + n] = 0.25
    query = np.zeros((2, 2, 4 * FEAT, WIDE), np.float32)
    key = np.zeros((2, 2, WIDE, 4 * FEAT), np.float32)
    pick = np.zeros((2, 4 * FEAT, 4 * FEAT), np.float32)
    for head in range(2):
        at = head * 2 * FEAT
        query[head, 0, at : at + FEAT] = first * weight
        query[head, 1, at : at + FEAT] = second
        key[head, 0, :, at + FEAT : at + 2 * FEAT] = first.T
        key[head, 1, :, at + FEAT : at + 2 * FEAT] = second.T
        pick[head, at : at + FEAT, at + FEAT : at + 2 * FEAT] = np.eye(FEAT)
    table = np.zeros((TABLE, WIDE), np.float32)
    table[0:256] = query.reshape(256, WIDE)
    table[256:1280, 0 : 4 * FEAT] = key.reshape(4 * WIDE, 4 * FEAT)
    table[1280:1408, 0 : 4 * FEAT] = pick.reshape(128, 4 * FEAT)
    return jnp.asarray(table, BF16)


def dot(a, b):
    return lax.dot_general(a, b, (((1,), (0,)), ((), ())), preferred_element_type=F32)


def dot_nt(a, b):
    return lax.dot_general(a, b, (((1,), (1,)), ((), ())), preferred_element_type=F32)


def factor_bias(shape, dim):
    p = lax.broadcasted_iota(jnp.int32, shape, dim)
    one = jnp.where(p == 19, 1.0, 0.0)
    two = jnp.where((p == 19) | (p % PART == 17) | (p % PART == 18), 1.0, 0.0)
    return one, two


def kernel(
    nctx, nz,
    tok, doc_in, wf_in, wv_in, ww_in, wo_in, table_in,
    out,
    doc, gath, wf, wv, ww, af, av, aw, table,
    feat, wq, kcat, vcat, docc, docr, fq, phiq,
    docs, lin, win, st_acc, st_send, st_recv, st_sums, st, mix, wo, sbuf, rbuf,
    load_sem, tok_sem, wo_sem, ring_send, ring_recv, par_send, par_recv,
    wo_send, wo_recv, doc_send, doc_recv, st_ssem, st_rsem, sum_ssem, sum_rsem, tail_send, tail_recv,
    mix_send, mix_recv, rs_send, rs_recv, told,
):
    n_sub = tok.shape[0] // SUB
    assert n_sub == 4
    units = n_sub * nz
    rows_total = tok.shape[0]
    part = WIDE // nctx
    b = lax.axis_index("ctx")
    head = lax.axis_index("head")
    z = head // 2
    k = head - 2 * z
    other = 1 - k
    way = 1 - 2 * k
    ahead = lax.rem(z + way + nz, nz) * 2 + k
    behind = lax.rem(z - way + nz, nz) * 2 + k
    partner = z * 2 + other

    far_first = sorted(range(1, nctx), key=lambda n: -min(n // 4, 4 - n // 4) - min(n % 4, 4 - n % 4))

    def sub_rows(i):
        return pl.ds(pl.multiple_of(i * SUB, SUB), SUB)

    def cols(block):
        return pl.ds(pl.multiple_of(block * 256, 256), 256)

    side = 4 if nctx > 4 else nctx
    base = b // side * side
    turns = [1] if side == 2 else [1, side - 1]
    beside = [base + lax.rem(b - base + n, side) for n in turns]
    if nctx > side:
        turns = [side] if nctx == 2 * side else [side, nctx - side]
        beside += [lax.rem(b + n, nctx) for n in turns]
    barrier = pltpu.get_barrier_semaphore()
    for peer in (ahead, behind, partner):
        pl.semaphore_signal(barrier, inc=1, device_id={"head": peer}, device_id_type=MESH)
    for peer in beside:
        pl.semaphore_signal(barrier, inc=1, device_id={"ctx": peer}, device_id_type=MESH)

    def tell(n):
        for peer in beside:
            pl.semaphore_signal(told.at[n], inc=1, device_id={"ctx": peer}, device_id_type=MESH)

    def hear(n):
        pl.semaphore_wait(told.at[n], len(beside))

    def bulk(ref, sem):
        return pltpu.make_async_copy(ref, ref, sem.at[0])

    loads = [
        pltpu.make_async_copy(src, dst, load_sem.at[n])
        for n, (src, dst) in enumerate(
            [(doc_in, doc), (wf_in, wf), (wv_in, wv), (ww_in, ww), (table_in, table)]
        )
    ]

    def tok_load(i):
        return pltpu.make_async_copy(tok.at[sub_rows(i)], gath.at[k, z, sub_rows(i)], tok_sem.at[i])

    for i in range(n_sub):
        tok_load(i).start()
    for load in loads:
        load.start()

    af[...] = jnp.zeros_like(af)
    av[...] = jnp.zeros_like(av)
    aw[...] = jnp.zeros_like(aw)
    st_acc[...] = jnp.zeros_like(st_acc)
    no_rows = jnp.zeros((LEAD - WIN, 256), BF16)
    for buf in (kcat, vcat):
        buf[0 : LEAD - WIN, :] = no_rows

    @pl.when(b == 0)
    def _():
        for buf in (kcat, vcat):
            buf[LEAD - WIN : LEAD, :] = no_rows

    pl.semaphore_wait(barrier, len(beside) + 3)

    def ring_copy(u):
        s = u // n_sub
        rows = sub_rows(u - s * n_sub)
        src = lax.rem(z - s * way + 2 * nz, nz)
        return pltpu.make_async_remote_copy(
            src_ref=gath.at[k, src, rows],
            dst_ref=gath.at[k, src, rows],
            send_sem=ring_send.at[0],
            recv_sem=ring_recv.at[u],
            device_id={"head": ahead},
            device_id_type=MESH,
        )

    def ring_arrival(u):
        s = u // n_sub
        rows = sub_rows(u - s * n_sub)
        src = lax.rem(z - s * way + 2 * nz, nz)
        slot = gath.at[k, src, rows]
        return pltpu.make_async_remote_copy(
            src_ref=slot,
            dst_ref=slot,
            send_sem=ring_send.at[0],
            recv_sem=ring_recv.at[u - n_sub],
            device_id={"head": ahead},
            device_id_type=MESH,
        )

    def par_copy(u, side, turn):
        s = u // n_sub
        rows = sub_rows(u - s * n_sub)
        src = lax.rem(z - s * turn + 2 * nz, nz)
        slot = gath.at[side, src, rows]
        return pltpu.make_async_remote_copy(
            src_ref=slot,
            dst_ref=slot,
            send_sem=par_send.at[0],
            recv_sem=par_recv.at[u],
            device_id={"head": partner},
            device_id_type=MESH,
        )

    def accumulate(u, side, turn, what="both"):
        s = u // n_sub
        rows = sub_rows(u - s * n_sub)
        src = lax.rem(z - s * turn + 2 * nz, nz)
        x = gath[side, src, rows, :]
        w_rows = cols(src * 2 + side)
        if what != "window":
            af[rows, :] += dot_nt(x, wf[:, w_rows])
            av[rows, :] += dot(x, wv[w_rows, :])
        if what != "state":
            aw[rows, :] += dot(x, ww[w_rows, :])

    for i in range(n_sub):
        tok_load(i).wait()
        ring_copy(i).start()
        par_copy(i, k, way).start()
    tell(0)

    loads[0].wait()

    def doc_copy(c, slot):
        return pltpu.make_async_remote_copy(
            src_ref=doc,
            dst_ref=docs.at[slot],
            send_sem=doc_send.at[0],
            recv_sem=doc_recv.at[0],
            device_id={"ctx": c},
            device_id_type=MESH,
        )

    def wo_copy(d, side, target):
        return pltpu.make_async_remote_copy(
            src_ref=wo_in.at[:, cols(d * 2 + target)],
            dst_ref=wo.at[side, d],
            send_sem=wo_send.at[0],
            recv_sem=wo_recv.at[0],
            device_id={"head": partner},
            device_id_type=MESH,
        )

    def wo_load(d):
        return pltpu.make_async_copy(wo_in.at[:, cols(d * 2 + k)], wo.at[k, d], wo_sem.at[0])


    def start_wo(d, carry):
        wo_copy(d, k, other).start()
        wo_load(d).start()
        return carry

    lax.fori_loop(0, nz, start_wo, 0)

    mine = doc[...].astype(F32)
    last_doc = mine[7:8, 127:128]
    for i in range(8):
        row = mine[i : i + 1, :]
        docr[0:1, LEAD + i * 128 : LEAD + (i + 1) * 128] = row
        docc[i * 128 : (i + 1) * 128, :] = jnp.broadcast_to(row, (128, 128)).T

    for load in loads[1:]:
        load.wait()

    lag = 6

    def own_unit(u, what="both"):
        @pl.when(u >= n_sub)
        def _():
            ring_arrival(u).wait_recv()

            @pl.when(u < units - n_sub)
            def _():
                ring_copy(u).start()

            par_copy(u, k, way).start()

        accumulate(u, k, way, what)

    def partner_unit(u, what="both"):
        par_copy(u, other, -way).wait_recv()
        accumulate(u, other, -way, what)

    def ring_step(u, carry):
        own_unit(u)

        @pl.when(u >= lag)
        def _():
            partner_unit(u - lag)

        return carry

    turn = units - n_sub
    lax.fori_loop(0, 2 * n_sub, ring_step, 0)
    hear(0)
    tell(1)
    lax.fori_loop(2 * n_sub, 3 * n_sub, ring_step, 0)
    hear(1)
    tell(2)
    lax.fori_loop(3 * n_sub, turn, ring_step, 0)
    hear(2)

    def start_doc(n, carry):
        doc_copy(lax.rem(b + n, nctx), b).start()
        return carry

    lax.fori_loop(1, nctx, start_doc, 0)

    one_k, two_k = factor_bias((WIDE, 1), 0)

    def finish(i):
        rows = sub_rows(i)
        late = pl.ds(pl.multiple_of(LEAD + i * SUB, 128), SUB)
        x = af[rows, :].astype(BF16)
        v = av[rows, :].astype(BF16)
        feat[rows, :] = x
        vcat[late, :] = v
        keeps = docr[0:1, late] == last_doc
        for j in range(2):
            at = 256 + 512 * j
            left = dot_nt(table[at : at + 256, 0:64], x) + one_k
            right = dot_nt(table[at + 256 : at + 512, 0:64], x) + two_k
            phi_k = jnp.where(keeps, left * right, 0.0).astype(BF16)
            st_acc[j] += dot(phi_k, v[:, j * 128 : (j + 1) * 128])

    def catch_up(n, carry):
        own_unit(turn + n)

        def partner_next(m, inner):
            partner_unit(turn - lag + 3 * n + m)
            return inner

        lax.fori_loop(0, 3, partner_next, 0)
        return carry

    def finish_early(n, carry):
        own_unit(turn + 2 + n, "state")
        partner_unit(turn + n, "state")
        finish(n)
        return carry

    def finish_late(n, carry):
        partner_unit(turn + 2 + n, "state")
        finish(2 + n)
        return carry

    lax.fori_loop(0, 2, catch_up, 0)
    lax.fori_loop(0, 2, finish_early, 0)
    lax.fori_loop(0, 2, finish_late, 0)

    def tail_copy(n):
        buf = (kcat, vcat)[n]
        return pltpu.make_async_remote_copy(
            src_ref=buf.at[LEAD + rows_total - WIN : LEAD + rows_total],
            dst_ref=buf.at[LEAD - WIN : LEAD],
            send_sem=tail_send.at[n],
            recv_sem=tail_recv.at[n],
            device_id={"ctx": lax.rem(b + 1, nctx)},
            device_id_type=MESH,
        )

    for j in range(2):
        st_send[:, j * part : (j + 1) * part, :] = st_acc[j].astype(BF16).reshape(nctx, part, 128)

    def st_copy(c, slot):
        return pltpu.make_async_remote_copy(
            src_ref=st_send.at[c],
            dst_ref=st_recv.at[slot],
            send_sem=st_ssem.at[0],
            recv_sem=st_rsem.at[0],
            device_id={"ctx": c},
            device_id_type=MESH,
        )

    for n in far_first:
        st_copy(lax.rem(b + n, nctx), b).start()

    def window_rows(i, carry):
        rows = sub_rows(i)
        late = pl.ds(pl.multiple_of(LEAD + i * SUB, 128), SUB)
        wq[rows, 0:128] = aw[rows, 0:128].astype(BF16)
        kcat[late, 0:128] = aw[rows, 128:256].astype(BF16)
        wq[rows, 128:256] = aw[rows, 256:384].astype(BF16)
        kcat[late, 128:256] = aw[rows, 384:512].astype(BF16)
        return carry

    def window_late(n, carry):
        accumulate(turn + 2 + n, k, way, "window")
        accumulate(turn + n, other, -way, "window")
        accumulate(turn + 2 + n, other, -way, "window")
        return carry

    lax.fori_loop(0, 2, window_late, 0)
    lax.fori_loop(0, n_sub, window_rows, 0)

    @pl.when(b < nctx - 1)
    def _():
        tail_copy(0).start()
        tail_copy(1).start()

    def feature_rows(i, carry):
        rows = sub_rows(i)
        x = feat[rows, :]
        for j in range(2):
            at = 1280 + 64 * j
            fq[j, rows, :] = dot(x, table[at : at + 64, 0:64]).astype(BF16)
        return carry

    lax.fori_loop(0, n_sub, feature_rows, 0)

    def taylor_rows(i):
        lo, hi = i * SUB, (i + 1) * SUB
        t_pos = lax.broadcasted_iota(jnp.int32, (SUB, hi), 0) + lo
        s_pos = lax.broadcasted_iota(jnp.int32, (SUB, hi), 1)
        allowed = (s_pos <= t_pos) & (docc[lo:hi, 0:1] == docr[0:1, LEAD : LEAD + hi])
        for j in range(2):
            d = dot_nt(fq[j, lo:hi, :], feat[0:hi, :])
            taylor = jnp.where(allowed, 1.0 + d * (0.25 + d * 0.03125), 0.0).astype(BF16)
            lin[lo:hi, j * 128 : (j + 1) * 128] = dot(
                taylor, vcat[LEAD : LEAD + hi, j * 128 : (j + 1) * 128]
            )

    taylor_rows(0)
    taylor_rows(1)

    def sum_back(c, slot):
        return pltpu.make_async_remote_copy(
            src_ref=st_sums.at[c],
            dst_ref=st.at[slot],
            send_sem=sum_ssem.at[0],
            recv_sem=sum_rsem.at[0],
            device_id={"ctx": c},
            device_id_type=MESH,
        )

    bulk(docs.at[0 : nctx - 1], doc_recv).wait()
    bulk(st_recv.at[0 : nctx - 1], st_rsem).wait()
    docs[b] = doc[...]
    st_recv[b] = st_send[b]

    sums = jnp.zeros((2 * part, 128), F32)
    for c in range(nctx - 1):
        same = docs[c][7:8, 127:128] == docs[max(c - 1, 0)][7:8, 127:128]
        sums = st_recv[c].astype(F32) + jnp.where(same, sums, 0.0)
        st_sums[c + 1] = sums.astype(BF16)

    def start_sum(c):
        @pl.when(c > 0)
        def _():
            sum_back(c, b).start()

    for n in far_first:
        start_sum(lax.rem(b + n, nctx))

    one_q, two_q = factor_bias((1, WIDE), 1)

    def query_rows(i, carry):
        rows = sub_rows(i)
        x = feat[rows, :]
        for j in range(2):
            left = dot(x, table[128 * j : 128 * j + 64, :]) + one_q
            right = dot(x, table[128 * j + 64 : 128 * j + 128, :]) + two_q
            phiq[j, rows, :] = (left * right).astype(BF16)
        return carry

    lax.fori_loop(0, n_sub, query_rows, 0)
    taylor_rows(2)

    @pl.when(b == 0)
    def _():
        docr[0:1, 0:LEAD] = jnp.full((1, LEAD), -1.0, F32)

    @pl.when(b > 0)
    def _():
        tail_copy(0).wait_recv()
        tail_copy(1).wait_recv()
        docr[0:1, 0:LEAD] = docs[b - 1][7:8, :].astype(F32)

    tile, reach = 128, LEAD + 128
    gap = lax.broadcasted_iota(jnp.int32, (tile, reach), 1) - lax.broadcasted_iota(
        jnp.int32, (tile, reach), 0
    )
    band = (gap > LEAD - WIN) & (gap <= LEAD)
    for i in range(rows_total // tile):
        lo, hi = i * tile, (i + 1) * tile
        within = band & (docc[lo:hi, 0:1] == docr[0:1, lo : lo + reach])
        for j in range(2):
            at = slice(j * 128, (j + 1) * 128)
            logits = jnp.where(within, dot_nt(wq[lo:hi, at], kcat[lo : lo + reach, at]), -1e30)
            top = jnp.max(logits, -1, keepdims=True)
            weights = jnp.exp((logits - top) * HEAD_DIM ** (-0.5))
            probs = (weights * (1.0 / jnp.sum(weights, -1, keepdims=True))).astype(BF16)
            win[lo:hi, at] = dot(probs, vcat[lo : lo + reach, at])

    @pl.when(b == 0)
    def _():
        st[...] = jnp.zeros_like(st)

    @pl.when(b > 0)
    def _():
        bulk(st.at[0 : nctx - 1], sum_rsem).wait()
        st[b] = st_sums[b]

    state = [
        st[:, j * part : (j + 1) * part, :].reshape(WIDE, 128) for j in range(2)
    ]

    def mix_copy(i, side):
        slot = mix.at[side, sub_rows(i)]
        return pltpu.make_async_remote_copy(
            src_ref=slot,
            dst_ref=slot,
            send_sem=mix_send.at[0],
            recv_sem=mix_recv.at[i],
            device_id={"head": partner},
            device_id_type=MESH,
        )

    def mix_rows(i, carry):
        rows = sub_rows(i)
        uses = docc[rows, :] == docr[0:1, LEAD - 1 : LEAD]
        for j in range(2):
            at = slice(j * 128, (j + 1) * 128)
            carried = dot(phiq[j, rows, :], state[j])
            linear = lin[rows, at] + jnp.where(uses, carried, 0.0)
            square = jnp.mean(linear * linear, -1, keepdims=True)
            normed = linear * lax.rsqrt(square + 1e-5)
            mix[k, rows, at] = (normed + win[rows, at]).astype(BF16)
        mix_copy(i, k).start()
        return carry


    bulk(wo.at[k], wo_sem).wait()
    bulk(wo.at[other], wo_recv).wait()

    def sum_copy(u):
        s = u // n_sub
        i = u - s * n_sub
        return pltpu.make_async_remote_copy(
            src_ref=sbuf.at[s, i],
            dst_ref=rbuf.at[s, i],
            send_sem=rs_send.at[0],
            recv_sem=rs_recv.at[u],
            device_id={"head": ahead},
            device_id_type=MESH,
        )

    def sum_step(u, carry):
        s = u // n_sub
        i = u - s * n_sub
        rows = sub_rows(i)
        dest = lax.rem(z - (s + 1) * way + 2 * nz, nz)

        @pl.when(u < n_sub)
        def _():
            mix_copy(i, other).wait_recv()

        part = dot(mix[0, rows, :], wo[0, dest]) + dot(mix[1, rows, :], wo[1, dest])

        @pl.when(u < n_sub)
        def _():
            sbuf[s, i] = part.astype(BF16)
            sum_copy(u).start()

        @pl.when(u >= n_sub)
        def _():
            sum_copy(u - n_sub).wait_recv()
            both = (part + rbuf[s - 1, i].astype(F32)).astype(BF16)

            @pl.when(u < units - n_sub)
            def _():
                sbuf[s, i] = both
                sum_copy(u).start()

            @pl.when(u >= units - n_sub)
            def _():
                out[rows, :] = both

        return carry

    def first_step(i, carry):
        @pl.when(i == n_sub - 1)
        def _():
            taylor_rows(n_sub - 1)

        @pl.when(i < n_sub)
        def _():
            mix_rows(i, 0)

        @pl.when(i > 0)
        def _():
            sum_step(i - 1, 0)

        return carry

    lax.fori_loop(0, n_sub + 1, first_step, 0)
    lax.fori_loop(n_sub, units, sum_step, 0)

    bulk(gath.at[k, 0 : nz - 1], ring_send).wait()
    bulk(gath.at[k], par_send).wait()
    bulk(sbuf, rs_send).wait()
    bulk(docs.at[0 : nctx - 1], doc_send).wait()
    bulk(st_send.at[0 : nctx - 1], st_ssem).wait()
    bulk(mix.at[k], mix_send).wait()
    bulk(wo.at[k], wo_send).wait()

    @pl.when(b == 0)
    def _():
        bulk(st_sums.at[0 : nctx - 1], sum_ssem).wait()

    @pl.when(b > 0)
    def _():
        bulk(st_sums.at[0 : nctx - 2], sum_ssem).wait()

    @pl.when(b < nctx - 1)
    def _():
        tail_copy(0).wait_send()
        tail_copy(1).wait_send()


def solution(mesh):
    nctx, nhead = mesh.shape["ctx"], mesh.shape["head"]
    nz = nhead // 2

    def shards(tokens, doc_ids, w_feat, w_value, w_window, w_out):
        rows = tokens.shape[0]
        width = w_value.shape[0]
        n_sub = rows // SUB
        units = n_sub * nz
        dma = pltpu.SemaphoreType.DMA
        vmem = pltpu.VMEM
        hbm_space = pl.BlockSpec(memory_space=pltpu.HBM)
        vmem_space = pl.BlockSpec(memory_space=pltpu.VMEM)
        return pl.pallas_call(
            functools.partial(kernel, nctx, nz),
            out_shape=jax.ShapeDtypeStruct((rows, 256), BF16),
            in_specs=[hbm_space] * 7,
            out_specs=vmem_space,
            scratch_shapes=[
                vmem((8, 128), jnp.int32),
                vmem((2, nz, rows, 256), BF16),
                vmem((64, width), BF16),
                vmem((width, 256), BF16),
                vmem((width, 512), BF16),
                vmem((rows, 64), F32),
                vmem((rows, 256), F32),
                vmem((rows, 512), F32),
                vmem((TABLE, WIDE), BF16),
                vmem((rows, 64), BF16),
                vmem((rows, 256), BF16),
                vmem((LEAD + rows, 256), BF16),
                vmem((LEAD + rows, 256), BF16),
                vmem((rows, 128), F32),
                vmem((1, LEAD + rows), F32),
                vmem((2, rows, 64), BF16),
                vmem((2, rows, WIDE), BF16),
                vmem((nctx, 8, 128), jnp.int32),
                vmem((rows, 256), F32),
                vmem((rows, 256), F32),
                vmem((2, WIDE, 128), F32),
                vmem((nctx, 2 * WIDE // nctx, 128), BF16),
                vmem((nctx, 2 * WIDE // nctx, 128), BF16),
                vmem((nctx, 2 * WIDE // nctx, 128), BF16),
                vmem((nctx, 2 * WIDE // nctx, 128), BF16),
                vmem((2, rows, 256), BF16),
                vmem((2, nz, 256, 256), BF16),
                vmem((nz - 1, n_sub, SUB, 256), BF16),
                vmem((nz - 1, n_sub, SUB, 256), BF16),
                dma((5,)),
                dma((n_sub,)),
                dma((1,)),
                dma((1,)),
                dma((units,)),
                dma((1,)),
                dma((units,)),
                dma((1,)),
                dma((1,)),
                dma((1,)),
                dma((1,)),
                dma((1,)),
                dma((1,)),
                dma((1,)),
                dma((1,)),
                dma((2,)),
                dma((2,)),
                dma((1,)),
                dma((n_sub,)),
                dma((1,)),
                dma((units - n_sub,)),
                pltpu.SemaphoreType.REGULAR((3,)),
            ],
            compiler_params=pltpu.CompilerParams(
                collective_id=0, has_side_effects=True, vmem_limit_bytes=67043328 - 11000 * 1024
            ),
            name="based_layer",
        )(
            tokens,
            pltpu.with_memory_space_constraint(doc_ids.reshape(8, 128), pltpu.HBM),
            w_feat.T,
            w_value,
            w_window,
            w_out,
            selection_tables(),
        )

    return jax.shard_map(
        shards,
        mesh=mesh,
        in_specs=(
            P("ctx", "head"),
            P("ctx"),
            P(None, "head"),
            P(None, "head"),
            P(None, "head"),
            P("head", None),
        ),
        out_specs=P("ctx", "head"),
        check_vma=False,
    )
```

```python
import functools

import jax
import jax.numpy as jnp
import numpy as np
from jax import lax
from jax.experimental import pallas as pl
from jax.experimental.pallas import tpu as pltpu
from jax.sharding import PartitionSpec as P

HEAD_DIM = 128
FEAT = 16
WIN = 64
SUB = 256
WIDE = 256
PACKED = 160
TABLE = 1024
LEAD = 128
F32 = jnp.float32
BF16 = jnp.bfloat16
MESH = pl.DeviceIdType.MESH


def selection_tables():
    first = np.zeros((FEAT, WIDE), np.float32)
    second = np.zeros((FEAT, WIDE), np.float32)
    weight = np.zeros((WIDE,), np.float32)
    for p in range(136):
        i, gap = p % FEAT, p // FEAT
        first[i, p] = 1.0
        second[(i + gap) % FEAT, p] = 1.0
        weight[p] = 1.0 / 32 if gap == 0 else 2.0 / 32
    for i in range(FEAT):
        first[i, 144 + i] = 1.0
        weight[144 + i] = 0.25
    query = np.zeros((2, 2, 4 * FEAT, WIDE), np.float32)
    key = np.zeros((2, 2, PACKED, 4 * FEAT), np.float32)
    pick = np.zeros((2, 4 * FEAT, 4 * FEAT), np.float32)
    for head in range(2):
        at = head * 2 * FEAT
        query[head, 0, at : at + FEAT] = first * weight
        query[head, 1, at : at + FEAT] = second
        key[head, 0, :, at + FEAT : at + 2 * FEAT] = first.T[:PACKED]
        key[head, 1, :, at + FEAT : at + 2 * FEAT] = second.T[:PACKED]
        pick[head, at : at + FEAT, at + FEAT : at + 2 * FEAT] = np.eye(FEAT)
    table = np.zeros((TABLE, WIDE), np.float32)
    table[0:256] = query.reshape(256, WIDE)
    table[256:896, 0 : 4 * FEAT] = key.reshape(4 * PACKED, 4 * FEAT)
    table[896:1024, 0 : 4 * FEAT] = pick.reshape(128, 4 * FEAT)
    return jnp.asarray(table, BF16)


def dot(a, b):
    return lax.dot_general(a, b, (((1,), (0,)), ((), ())), preferred_element_type=F32)


def dot_nt(a, b):
    return lax.dot_general(a, b, (((1,), (1,)), ((), ())), preferred_element_type=F32)


def factor_bias(shape, dim):
    p = lax.broadcasted_iota(jnp.int32, shape, dim)
    one = jnp.where(p == 136, 1.0, 0.0)
    two = jnp.where((p == 136) | ((p >= 144) & (p < 160)), 1.0, 0.0)
    return one, two


def kernel(
    nctx, nz,
    tok, doc_in, wf_in, wv_in, ww_in, wo_in, table_in,
    out,
    doc, gath, wf, wv, ww, af, av, aw, table,
    feat, wq, kcat, vcat, docc, docr, fq, phiq,
    docs, lin, win, st_acc, st_send, st_recv, st_sums, st, mix, wo, sbuf, rbuf,
    load_sem, tok_sem, wo_sem, ring_send, ring_recv, par_send, par_recv,
    wo_send, wo_recv, doc_send, doc_recv, st_ssem, st_rsem, sum_ssem, sum_rsem, tail_send, tail_recv,
    mix_send, mix_recv, rs_send, rs_recv, told,
):
    n_sub = tok.shape[0] // SUB
    assert n_sub == 4
    units = n_sub * nz
    rows_total = tok.shape[0]
    owners = st.shape[0]
    part = PACKED // owners
    b = lax.axis_index("ctx")
    head = lax.axis_index("head")
    z = head // 2
    k = head - 2 * z
    other = 1 - k
    way = 1 - 2 * k
    ahead = lax.rem(z + way + nz, nz) * 2 + k
    behind = lax.rem(z - way + nz, nz) * 2 + k
    partner = z * 2 + other

    far_first = sorted(range(1, nctx), key=lambda n: -min(n // 4, 4 - n // 4) - min(n % 4, 4 - n % 4))

    def sub_rows(i):
        return pl.ds(pl.multiple_of(i * SUB, SUB), SUB)

    def cols(block):
        return pl.ds(pl.multiple_of(block * 256, 256), 256)

    side = 4 if nctx > 4 else nctx
    base = b // side * side
    turns = [1] if side == 2 else [1, side - 1]
    beside = [base + lax.rem(b - base + n, side) for n in turns]
    if nctx > side:
        turns = [side] if nctx == 2 * side else [side, nctx - side]
        beside += [lax.rem(b + n, nctx) for n in turns]
    barrier = pltpu.get_barrier_semaphore()
    for peer in (ahead, behind, partner):
        pl.semaphore_signal(barrier, inc=1, device_id={"head": peer}, device_id_type=MESH)
    for peer in beside:
        pl.semaphore_signal(barrier, inc=1, device_id={"ctx": peer}, device_id_type=MESH)

    def tell(n):
        for peer in beside:
            pl.semaphore_signal(told.at[n], inc=1, device_id={"ctx": peer}, device_id_type=MESH)

    def hear(n):
        pl.semaphore_wait(told.at[n], len(beside))

    def bulk(ref, sem):
        return pltpu.make_async_copy(ref, ref, sem.at[0])

    loads = [
        pltpu.make_async_copy(src, dst, load_sem.at[n])
        for n, (src, dst) in enumerate(
            [(doc_in, doc), (wf_in, wf), (wv_in, wv), (ww_in, ww), (table_in, table)]
        )
    ]

    def tok_load(i):
        return pltpu.make_async_copy(tok.at[sub_rows(i)], gath.at[k, z, sub_rows(i)], tok_sem.at[i])

    for i in range(n_sub):
        tok_load(i).start()
    for load in loads:
        load.start()

    af[...] = jnp.zeros_like(af)
    av[...] = jnp.zeros_like(av)
    aw[...] = jnp.zeros_like(aw)
    st_acc[...] = jnp.zeros_like(st_acc)
    no_rows = jnp.zeros((LEAD - WIN, 256), BF16)
    for buf in (kcat, vcat):
        buf[0 : LEAD - WIN, :] = no_rows

    @pl.when(b == 0)
    def _():
        for buf in (kcat, vcat):
            buf[LEAD - WIN : LEAD, :] = no_rows

    pl.semaphore_wait(barrier, len(beside) + 3)

    def ring_copy(u):
        s = u // n_sub
        rows = sub_rows(u - s * n_sub)
        src = lax.rem(z - s * way + 2 * nz, nz)
        return pltpu.make_async_remote_copy(
            src_ref=gath.at[k, src, rows],
            dst_ref=gath.at[k, src, rows],
            send_sem=ring_send.at[0],
            recv_sem=ring_recv.at[u],
            device_id={"head": ahead},
            device_id_type=MESH,
        )

    def ring_arrival(u):
        s = u // n_sub
        rows = sub_rows(u - s * n_sub)
        src = lax.rem(z - s * way + 2 * nz, nz)
        slot = gath.at[k, src, rows]
        return pltpu.make_async_remote_copy(
            src_ref=slot,
            dst_ref=slot,
            send_sem=ring_send.at[0],
            recv_sem=ring_recv.at[u - n_sub],
            device_id={"head": ahead},
            device_id_type=MESH,
        )

    def par_copy(u, side, turn):
        s = u // n_sub
        rows = sub_rows(u - s * n_sub)
        src = lax.rem(z - s * turn + 2 * nz, nz)
        slot = gath.at[side, src, rows]
        return pltpu.make_async_remote_copy(
            src_ref=slot,
            dst_ref=slot,
            send_sem=par_send.at[0],
            recv_sem=par_recv.at[u],
            device_id={"head": partner},
            device_id_type=MESH,
        )

    def accumulate(u, side, turn, what="both"):
        s = u // n_sub
        rows = sub_rows(u - s * n_sub)
        src = lax.rem(z - s * turn + 2 * nz, nz)
        x = gath[side, src, rows, :]
        w_rows = cols(src * 2 + side)
        if what != "window":
            af[rows, :] += dot_nt(x, wf[:, w_rows])
            av[rows, :] += dot(x, wv[w_rows, :])
        if what != "state":
            aw[rows, :] += dot(x, ww[w_rows, :])

    for i in range(n_sub):
        tok_load(i).wait()
        ring_copy(i).start()
        par_copy(i, k, way).start()
    tell(0)

    loads[0].wait()

    def doc_copy(c, slot):
        return pltpu.make_async_remote_copy(
            src_ref=doc,
            dst_ref=docs.at[slot],
            send_sem=doc_send.at[0],
            recv_sem=doc_recv.at[0],
            device_id={"ctx": c},
            device_id_type=MESH,
        )

    def wo_copy(d, side, target):
        return pltpu.make_async_remote_copy(
            src_ref=wo_in.at[:, cols(d * 2 + target)],
            dst_ref=wo.at[side, d],
            send_sem=wo_send.at[0],
            recv_sem=wo_recv.at[0],
            device_id={"head": partner},
            device_id_type=MESH,
        )

    def wo_load(d):
        return pltpu.make_async_copy(wo_in.at[:, cols(d * 2 + k)], wo.at[k, d], wo_sem.at[0])


    def start_wo(d, carry):
        wo_copy(d, k, other).start()
        wo_load(d).start()
        return carry

    lax.fori_loop(0, nz, start_wo, 0)

    mine = doc[...].astype(F32)
    last_doc = mine[7:8, 127:128]
    for i in range(8):
        row = mine[i : i + 1, :]
        docr[0:1, LEAD + i * 128 : LEAD + (i + 1) * 128] = row
        docc[i * 128 : (i + 1) * 128, :] = jnp.broadcast_to(row, (128, 128)).T

    for load in loads[1:]:
        load.wait()

    lag = 6

    def own_unit(u, what="both"):
        @pl.when(u >= n_sub)
        def _():
            ring_arrival(u).wait_recv()

            @pl.when(u < units - n_sub)
            def _():
                ring_copy(u).start()

            par_copy(u, k, way).start()

        accumulate(u, k, way, what)

    def partner_unit(u, what="both"):
        par_copy(u, other, -way).wait_recv()
        accumulate(u, other, -way, what)

    def ring_step(u, carry):
        own_unit(u)

        @pl.when(u >= lag)
        def _():
            partner_unit(u - lag)

        return carry

    turn = units - n_sub
    lax.fori_loop(0, 2 * n_sub, ring_step, 0)
    hear(0)
    tell(1)
    lax.fori_loop(2 * n_sub, 3 * n_sub, ring_step, 0)
    hear(1)
    tell(2)
    lax.fori_loop(3 * n_sub, turn, ring_step, 0)
    hear(2)

    def start_doc(n, carry):
        doc_copy(lax.rem(b + n, nctx), b).start()
        return carry

    lax.fori_loop(1, nctx, start_doc, 0)

    one_k, two_k = factor_bias((PACKED, 1), 0)

    def finish(i):
        rows = sub_rows(i)
        late = pl.ds(pl.multiple_of(LEAD + i * SUB, 128), SUB)
        x = af[rows, :].astype(BF16)
        v = av[rows, :].astype(BF16)
        feat[rows, :] = x
        vcat[late, :] = v
        keeps = docr[0:1, late] == last_doc
        for j in range(2):
            at = 256 + 2 * PACKED * j
            left = dot_nt(table[at : at + PACKED, 0:64], x) + one_k
            right = dot_nt(table[at + PACKED : at + 2 * PACKED, 0:64], x) + two_k
            phi_k = jnp.where(keeps, left * right, 0.0).astype(BF16)
            st_acc[j] += dot(phi_k, v[:, j * 128 : (j + 1) * 128])

    def catch_up(n, carry):
        own_unit(turn + n)

        def partner_next(m, inner):
            partner_unit(turn - lag + 3 * n + m)
            return inner

        lax.fori_loop(0, 3, partner_next, 0)
        return carry

    def finish_early(n, carry):
        own_unit(turn + 2 + n, "state")
        partner_unit(turn + n, "state")
        finish(n)
        return carry

    def finish_late(n, carry):
        partner_unit(turn + 2 + n, "state")
        finish(2 + n)
        return carry

    lax.fori_loop(0, 2, catch_up, 0)
    lax.fori_loop(0, 2, finish_early, 0)
    lax.fori_loop(0, 2, finish_late, 0)

    def tail_copy(n):
        buf = (kcat, vcat)[n]
        return pltpu.make_async_remote_copy(
            src_ref=buf.at[LEAD + rows_total - WIN : LEAD + rows_total],
            dst_ref=buf.at[LEAD - WIN : LEAD],
            send_sem=tail_send.at[n],
            recv_sem=tail_recv.at[n],
            device_id={"ctx": lax.rem(b + 1, nctx)},
            device_id_type=MESH,
        )

    for j in range(2):
        st_send[:, j * part : (j + 1) * part, :] = st_acc[j].astype(BF16).reshape(owners, part, 128)

    def st_copy(c, slot):
        return pltpu.make_async_remote_copy(
            src_ref=st_send.at[c],
            dst_ref=st_recv.at[slot],
            send_sem=st_ssem.at[0],
            recv_sem=st_rsem.at[0],
            device_id={"ctx": c},
            device_id_type=MESH,
        )

    def start_state(c):
        @pl.when(c < owners)
        def _():
            st_copy(c, b).start()

    for n in far_first:
        start_state(lax.rem(b + n, nctx))

    def window_rows(i, carry):
        rows = sub_rows(i)
        late = pl.ds(pl.multiple_of(LEAD + i * SUB, 128), SUB)
        wq[rows, 0:128] = aw[rows, 0:128].astype(BF16)
        kcat[late, 0:128] = aw[rows, 128:256].astype(BF16)
        wq[rows, 128:256] = aw[rows, 256:384].astype(BF16)
        kcat[late, 128:256] = aw[rows, 384:512].astype(BF16)
        return carry

    def window_late(n, carry):
        accumulate(turn + 2 + n, k, way, "window")
        accumulate(turn + n, other, -way, "window")
        accumulate(turn + 2 + n, other, -way, "window")
        return carry

    lax.fori_loop(0, 2, window_late, 0)
    lax.fori_loop(0, n_sub, window_rows, 0)

    @pl.when(b < nctx - 1)
    def _():
        tail_copy(0).start()
        tail_copy(1).start()

    def feature_rows(i, carry):
        rows = sub_rows(i)
        x = feat[rows, :]
        for j in range(2):
            at = 896 + 64 * j
            fq[j, rows, :] = dot(x, table[at : at + 64, 0:64]).astype(BF16)
        return carry

    lax.fori_loop(0, n_sub, feature_rows, 0)

    def taylor_rows(i):
        lo, hi = i * SUB, (i + 1) * SUB
        t_pos = lax.broadcasted_iota(jnp.int32, (SUB, hi), 0) + lo
        s_pos = lax.broadcasted_iota(jnp.int32, (SUB, hi), 1)
        allowed = (s_pos <= t_pos) & (docc[lo:hi, 0:1] == docr[0:1, LEAD : LEAD + hi])
        for j in range(2):
            d = dot_nt(fq[j, lo:hi, :], feat[0:hi, :])
            taylor = jnp.where(allowed, 1.0 + d * (0.25 + d * 0.03125), 0.0).astype(BF16)
            lin[lo:hi, j * 128 : (j + 1) * 128] = dot(
                taylor, vcat[LEAD : LEAD + hi, j * 128 : (j + 1) * 128]
            )

    taylor_rows(0)
    taylor_rows(1)

    def sum_back(c, slot):
        return pltpu.make_async_remote_copy(
            src_ref=st_sums.at[c],
            dst_ref=st.at[slot],
            send_sem=sum_ssem.at[0],
            recv_sem=sum_rsem.at[0],
            device_id={"ctx": c},
            device_id_type=MESH,
        )

    bulk(docs.at[0 : nctx - 1], doc_recv).wait()
    docs[b] = doc[...]

    def start_sum(c):
        @pl.when(c > 0)
        def _():
            sum_back(c, b).start()

    @pl.when(b < owners)
    def _():
        bulk(st_recv.at[0 : nctx - 1], st_rsem).wait()
        st_recv[b] = st_send[b]
        sums = jnp.zeros((2 * part, 128), F32)
        for c in range(nctx - 1):
            same = docs[c][7:8, 127:128] == docs[max(c - 1, 0)][7:8, 127:128]
            sums = st_recv[c].astype(F32) + jnp.where(same, sums, 0.0)
            st_sums[c + 1] = sums.astype(BF16)
        for n in far_first:
            start_sum(lax.rem(b + n, nctx))

    one_q, two_q = factor_bias((1, WIDE), 1)

    def query_rows(i, carry):
        rows = sub_rows(i)
        x = feat[rows, :]
        for j in range(2):
            left = dot(x, table[128 * j : 128 * j + 64, :]) + one_q
            right = dot(x, table[128 * j + 64 : 128 * j + 128, :]) + two_q
            phiq[j, rows, :] = (left * right).astype(BF16)
        return carry

    lax.fori_loop(0, n_sub, query_rows, 0)
    taylor_rows(2)

    @pl.when(b == 0)
    def _():
        docr[0:1, 0:LEAD] = jnp.full((1, LEAD), -1.0, F32)

    @pl.when(b > 0)
    def _():
        tail_copy(0).wait_recv()
        tail_copy(1).wait_recv()
        docr[0:1, 0:LEAD] = docs[b - 1][7:8, :].astype(F32)

    tile, reach = 128, LEAD + 128
    gap = lax.broadcasted_iota(jnp.int32, (tile, reach), 1) - lax.broadcasted_iota(
        jnp.int32, (tile, reach), 0
    )
    band = (gap > LEAD - WIN) & (gap <= LEAD)
    for i in range(rows_total // tile):
        lo, hi = i * tile, (i + 1) * tile
        within = band & (docc[lo:hi, 0:1] == docr[0:1, lo : lo + reach])
        for j in range(2):
            at = slice(j * 128, (j + 1) * 128)
            logits = jnp.where(within, dot_nt(wq[lo:hi, at], kcat[lo : lo + reach, at]), -1e30)
            top = jnp.max(logits, -1, keepdims=True)
            weights = jnp.exp((logits - top) * HEAD_DIM ** (-0.5))
            probs = (weights * (1.0 / jnp.sum(weights, -1, keepdims=True))).astype(BF16)
            win[lo:hi, at] = dot(probs, vcat[lo : lo + reach, at])

    @pl.when(b == 0)
    def _():
        st[...] = jnp.zeros_like(st)

    @pl.when((b > 0) & (b < owners))
    def _():
        bulk(st.at[0 : owners - 1], sum_rsem).wait()
        st[b] = st_sums[b]

    @pl.when((b > 0) & (b >= owners))
    def _():
        bulk(st, sum_rsem).wait()

    rest = jnp.zeros((WIDE - PACKED, 128), BF16)
    state = [
        jnp.concatenate([st[:, j * part : (j + 1) * part, :].reshape(PACKED, 128), rest], 0)
        for j in range(2)
    ]

    def mix_copy(i, side):
        slot = mix.at[side, sub_rows(i)]
        return pltpu.make_async_remote_copy(
            src_ref=slot,
            dst_ref=slot,
            send_sem=mix_send.at[0],
            recv_sem=mix_recv.at[i],
            device_id={"head": partner},
            device_id_type=MESH,
        )

    def mix_rows(i, carry):
        rows = sub_rows(i)
        uses = docc[rows, :] == docr[0:1, LEAD - 1 : LEAD]
        for j in range(2):
            at = slice(j * 128, (j + 1) * 128)
            carried = dot(phiq[j, rows, :], state[j])
            linear = lin[rows, at] + jnp.where(uses, carried, 0.0)
            square = jnp.mean(linear * linear, -1, keepdims=True)
            normed = linear * lax.rsqrt(square + 1e-5)
            mix[k, rows, at] = (normed + win[rows, at]).astype(BF16)
        mix_copy(i, k).start()
        return carry


    bulk(wo.at[k], wo_sem).wait()
    bulk(wo.at[other], wo_recv).wait()

    def sum_copy(u):
        s = u // n_sub
        i = u - s * n_sub
        return pltpu.make_async_remote_copy(
            src_ref=sbuf.at[s, i],
            dst_ref=rbuf.at[s, i],
            send_sem=rs_send.at[0],
            recv_sem=rs_recv.at[u],
            device_id={"head": ahead},
            device_id_type=MESH,
        )

    def sum_step(u, carry):
        s = u // n_sub
        i = u - s * n_sub
        rows = sub_rows(i)
        dest = lax.rem(z - (s + 1) * way + 2 * nz, nz)

        @pl.when(u < n_sub)
        def _():
            mix_copy(i, other).wait_recv()

        part = dot(mix[0, rows, :], wo[0, dest]) + dot(mix[1, rows, :], wo[1, dest])

        @pl.when(u < n_sub)
        def _():
            sbuf[s, i] = part.astype(BF16)
            sum_copy(u).start()

        @pl.when(u >= n_sub)
        def _():
            sum_copy(u - n_sub).wait_recv()
            both = (part + rbuf[s - 1, i].astype(F32)).astype(BF16)

            @pl.when(u < units - n_sub)
            def _():
                sbuf[s, i] = both
                sum_copy(u).start()

            @pl.when(u >= units - n_sub)
            def _():
                out[rows, :] = both

        return carry

    def first_step(i, carry):
        @pl.when(i == n_sub - 1)
        def _():
            taylor_rows(n_sub - 1)

        @pl.when(i < n_sub)
        def _():
            mix_rows(i, 0)

        @pl.when(i > 0)
        def _():
            sum_step(i - 1, 0)

        return carry

    lax.fori_loop(0, n_sub + 1, first_step, 0)
    lax.fori_loop(n_sub, units, sum_step, 0)

    bulk(gath.at[k, 0 : nz - 1], ring_send).wait()
    bulk(gath.at[k], par_send).wait()
    bulk(sbuf, rs_send).wait()
    bulk(docs.at[0 : nctx - 1], doc_send).wait()
    bulk(mix.at[k], mix_send).wait()
    bulk(wo.at[k], wo_send).wait()

    @pl.when(b < owners)
    def _():
        bulk(st_send.at[0 : owners - 1], st_ssem).wait()

    @pl.when(b >= owners)
    def _():
        bulk(st_send, st_ssem).wait()

    @pl.when(b == 0)
    def _():
        bulk(st_sums.at[0 : nctx - 1], sum_ssem).wait()

    @pl.when((b > 0) & (b < owners))
    def _():
        bulk(st_sums.at[0 : nctx - 2], sum_ssem).wait()

    @pl.when(b < nctx - 1)
    def _():
        tail_copy(0).wait_send()
        tail_copy(1).wait_send()


def solution(mesh):
    nctx, nhead = mesh.shape["ctx"], mesh.shape["head"]
    nz = nhead // 2

    def shards(tokens, doc_ids, w_feat, w_value, w_window, w_out):
        rows = tokens.shape[0]
        width = w_value.shape[0]
        n_sub = rows // SUB
        units = n_sub * nz
        owners = min(nctx, 10)
        dma = pltpu.SemaphoreType.DMA
        vmem = pltpu.VMEM
        hbm_space = pl.BlockSpec(memory_space=pltpu.HBM)
        vmem_space = pl.BlockSpec(memory_space=pltpu.VMEM)
        return pl.pallas_call(
            functools.partial(kernel, nctx, nz),
            out_shape=jax.ShapeDtypeStruct((rows, 256), BF16),
            in_specs=[hbm_space] * 7,
            out_specs=vmem_space,
            scratch_shapes=[
                vmem((8, 128), jnp.int32),
                vmem((2, nz, rows, 256), BF16),
                vmem((64, width), BF16),
                vmem((width, 256), BF16),
                vmem((width, 512), BF16),
                vmem((rows, 64), F32),
                vmem((rows, 256), F32),
                vmem((rows, 512), F32),
                vmem((TABLE, WIDE), BF16),
                vmem((rows, 64), BF16),
                vmem((rows, 256), BF16),
                vmem((LEAD + rows, 256), BF16),
                vmem((LEAD + rows, 256), BF16),
                vmem((rows, 128), F32),
                vmem((1, LEAD + rows), F32),
                vmem((2, rows, 64), BF16),
                vmem((2, rows, WIDE), BF16),
                vmem((nctx, 8, 128), jnp.int32),
                vmem((rows, 256), F32),
                vmem((rows, 256), F32),
                vmem((2, PACKED, 128), F32),
                vmem((owners, 2 * PACKED // owners, 128), BF16),
                vmem((nctx, 2 * PACKED // owners, 128), BF16),
                vmem((nctx, 2 * PACKED // owners, 128), BF16),
                vmem((owners, 2 * PACKED // owners, 128), BF16),
                vmem((2, rows, 256), BF16),
                vmem((2, nz, 256, 256), BF16),
                vmem((nz - 1, n_sub, SUB, 256), BF16),
                vmem((nz - 1, n_sub, SUB, 256), BF16),
                dma((5,)),
                dma((n_sub,)),
                dma((1,)),
                dma((1,)),
                dma((units,)),
                dma((1,)),
                dma((units,)),
                dma((1,)),
                dma((1,)),
                dma((1,)),
                dma((1,)),
                dma((1,)),
                dma((1,)),
                dma((1,)),
                dma((1,)),
                dma((2,)),
                dma((2,)),
                dma((1,)),
                dma((n_sub,)),
                dma((1,)),
                dma((units - n_sub,)),
                pltpu.SemaphoreType.REGULAR((3,)),
            ],
            compiler_params=pltpu.CompilerParams(
                collective_id=0, has_side_effects=True, vmem_limit_bytes=67043328 - 11000 * 1024
            ),
            name="based_layer",
        )(
            tokens,
            pltpu.with_memory_space_constraint(doc_ids.reshape(8, 128), pltpu.HBM),
            w_feat.T,
            w_value,
            w_window,
            w_out,
            selection_tables(),
        )

    return jax.shard_map(
        shards,
        mesh=mesh,
        in_specs=(
            P("ctx", "head"),
            P("ctx"),
            P(None, "head"),
            P(None, "head"),
            P(None, "head"),
            P("head", None),
        ),
        out_specs=P("ctx", "head"),
        check_vma=False,
    )
```

```python
import functools

import jax
import jax.numpy as jnp
import numpy as np
from jax import lax
from jax.experimental import pallas as pl
from jax.experimental.pallas import tpu as pltpu
from jax.sharding import PartitionSpec as P

HEAD_DIM = 128
FEAT = 16
WIN = 64
SUB = 256
WIDE = 256
PACKED = 160
TABLE = 1024
LEAD = 128
F32 = jnp.float32
BF16 = jnp.bfloat16
MESH = pl.DeviceIdType.MESH


def selection_tables():
    first = np.zeros((FEAT, WIDE), np.float32)
    second = np.zeros((FEAT, WIDE), np.float32)
    weight = np.zeros((WIDE,), np.float32)
    for p in range(136):
        i, gap = p % FEAT, p // FEAT
        first[i, p] = 1.0
        second[(i + gap) % FEAT, p] = 1.0
        weight[p] = 1.0 / 32 if gap == 0 else 2.0 / 32
    for i in range(FEAT):
        first[i, 144 + i] = 1.0
        weight[144 + i] = 0.25
    query = np.zeros((2, 2, 4 * FEAT, WIDE), np.float32)
    key = np.zeros((2, 2, PACKED, 4 * FEAT), np.float32)
    pick = np.zeros((2, 4 * FEAT, 4 * FEAT), np.float32)
    for head in range(2):
        at = head * 2 * FEAT
        query[head, 0, at : at + FEAT] = first * weight
        query[head, 1, at : at + FEAT] = second
        key[head, 0, :, at + FEAT : at + 2 * FEAT] = first.T[:PACKED]
        key[head, 1, :, at + FEAT : at + 2 * FEAT] = second.T[:PACKED]
        pick[head, at : at + FEAT, at + FEAT : at + 2 * FEAT] = np.eye(FEAT)
    table = np.zeros((TABLE, WIDE), np.float32)
    table[0:256] = query.reshape(256, WIDE)
    table[256:896, 0 : 4 * FEAT] = key.reshape(4 * PACKED, 4 * FEAT)
    table[896:1024, 0 : 4 * FEAT] = pick.reshape(128, 4 * FEAT)
    return jnp.asarray(table, BF16)


def dot(a, b):
    return lax.dot_general(a, b, (((1,), (0,)), ((), ())), preferred_element_type=F32)


def dot_nt(a, b):
    return lax.dot_general(a, b, (((1,), (1,)), ((), ())), preferred_element_type=F32)


def factor_bias(shape, dim):
    p = lax.broadcasted_iota(jnp.int32, shape, dim)
    one = jnp.where(p == 136, 1.0, 0.0)
    two = jnp.where((p == 136) | ((p >= 144) & (p < 160)), 1.0, 0.0)
    return one, two


def kernel(
    nctx, nz,
    tok, doc_in, wf_in, wv_in, ww_in, wo_in, table_in,
    out,
    doc, gath, wf, wv, ww, af, av, aw, table,
    feat, wq, kcat, vcat, docc, docr, fq, phiq,
    docs, lin, win, st_acc, st_send, st_recv, st_sums, st, mix, wo, sbuf, rbuf,
    load_sem, tok_sem, wo_sem, ring_send, ring_recv, par_send, par_recv,
    wo_send, wo_recv, doc_send, doc_recv, st_ssem, st_rsem, sum_ssem, sum_rsem, tail_send, tail_recv,
    mix_send, mix_recv, rs_send, rs_recv, told,
):
    n_sub = tok.shape[0] // SUB
    assert n_sub == 4
    units = n_sub * nz
    rows_total = tok.shape[0]
    owners = st.shape[0]
    part = PACKED // owners
    b = lax.axis_index("ctx")
    head = lax.axis_index("head")
    z = head // 2
    k = head - 2 * z
    other = 1 - k
    way = 1 - 2 * k
    ahead = lax.rem(z + way + nz, nz) * 2 + k
    behind = lax.rem(z - way + nz, nz) * 2 + k
    partner = z * 2 + other

    far_first = sorted(range(1, nctx), key=lambda n: -min(n // 4, 4 - n // 4) - min(n % 4, 4 - n % 4))

    def sub_rows(i):
        return pl.ds(pl.multiple_of(i * SUB, SUB), SUB)

    def cols(block):
        return pl.ds(pl.multiple_of(block * 256, 256), 256)

    side = 4 if nctx > 4 else nctx
    base = b // side * side
    turns = [1] if side == 2 else [1, side - 1]
    beside = [base + lax.rem(b - base + n, side) for n in turns]
    if nctx > side:
        turns = [side] if nctx == 2 * side else [side, nctx - side]
        beside += [lax.rem(b + n, nctx) for n in turns]
    barrier = pltpu.get_barrier_semaphore()
    for peer in (ahead, behind, partner):
        pl.semaphore_signal(barrier, inc=1, device_id={"head": peer}, device_id_type=MESH)
    for peer in beside:
        pl.semaphore_signal(barrier, inc=1, device_id={"ctx": peer}, device_id_type=MESH)

    def tell(n):
        for peer in beside:
            pl.semaphore_signal(told.at[n], inc=1, device_id={"ctx": peer}, device_id_type=MESH)

    def hear(n):
        pl.semaphore_wait(told.at[n], len(beside))

    def bulk(ref, sem):
        return pltpu.make_async_copy(ref, ref, sem.at[0])

    loads = [
        pltpu.make_async_copy(src, dst, load_sem.at[n])
        for n, (src, dst) in enumerate(
            [(doc_in, doc), (wf_in, wf), (wv_in, wv), (ww_in, ww), (table_in, table)]
        )
    ]

    def tok_load(i):
        return pltpu.make_async_copy(tok.at[sub_rows(i)], gath.at[k, z, sub_rows(i)], tok_sem.at[i])

    for i in range(n_sub):
        tok_load(i).start()
    for load in loads:
        load.start()

    af[...] = jnp.zeros_like(af)
    av[...] = jnp.zeros_like(av)
    aw[...] = jnp.zeros_like(aw)
    st_acc[...] = jnp.zeros_like(st_acc)
    no_rows = jnp.zeros((LEAD - WIN, 256), BF16)
    for buf in (kcat, vcat):
        buf[0 : LEAD - WIN, :] = no_rows

    @pl.when(b == 0)
    def _():
        for buf in (kcat, vcat):
            buf[LEAD - WIN : LEAD, :] = no_rows

    pl.semaphore_wait(barrier, len(beside) + 3)

    def ring_copy(u):
        s = u // n_sub
        rows = sub_rows(u - s * n_sub)
        src = lax.rem(z - s * way + 2 * nz, nz)
        return pltpu.make_async_remote_copy(
            src_ref=gath.at[k, src, rows],
            dst_ref=gath.at[k, src, rows],
            send_sem=ring_send.at[0],
            recv_sem=ring_recv.at[u],
            device_id={"head": ahead},
            device_id_type=MESH,
        )

    def ring_arrival(u):
        s = u // n_sub
        rows = sub_rows(u - s * n_sub)
        src = lax.rem(z - s * way + 2 * nz, nz)
        slot = gath.at[k, src, rows]
        return pltpu.make_async_remote_copy(
            src_ref=slot,
            dst_ref=slot,
            send_sem=ring_send.at[0],
            recv_sem=ring_recv.at[u - n_sub],
            device_id={"head": ahead},
            device_id_type=MESH,
        )

    def par_copy(u, side, turn):
        s = u // n_sub
        rows = sub_rows(u - s * n_sub)
        src = lax.rem(z - s * turn + 2 * nz, nz)
        slot = gath.at[side, src, rows]
        return pltpu.make_async_remote_copy(
            src_ref=slot,
            dst_ref=slot,
            send_sem=par_send.at[0],
            recv_sem=par_recv.at[u],
            device_id={"head": partner},
            device_id_type=MESH,
        )

    def accumulate(u, side, turn, what="both"):
        s = u // n_sub
        rows = sub_rows(u - s * n_sub)
        src = lax.rem(z - s * turn + 2 * nz, nz)
        x = gath[side, src, rows, :]
        w_rows = cols(src * 2 + side)
        if what != "window":
            af[rows, :] += dot_nt(x, wf[:, w_rows])
            av[rows, :] += dot(x, wv[w_rows, :])
        if what != "state":
            aw[rows, :] += dot(x, ww[w_rows, :])

    for i in range(n_sub):
        tok_load(i).wait()
        ring_copy(i).start()
        par_copy(i, k, way).start()
    tell(0)

    loads[0].wait()

    def doc_copy(c, slot):
        return pltpu.make_async_remote_copy(
            src_ref=doc,
            dst_ref=docs.at[slot],
            send_sem=doc_send.at[0],
            recv_sem=doc_recv.at[0],
            device_id={"ctx": c},
            device_id_type=MESH,
        )

    def wo_copy(d, side, target):
        return pltpu.make_async_remote_copy(
            src_ref=wo_in.at[:, cols(d * 2 + target)],
            dst_ref=wo.at[side, d],
            send_sem=wo_send.at[0],
            recv_sem=wo_recv.at[0],
            device_id={"head": partner},
            device_id_type=MESH,
        )

    def wo_load(d):
        return pltpu.make_async_copy(wo_in.at[:, cols(d * 2 + k)], wo.at[k, d], wo_sem.at[0])


    def start_wo(d, carry):
        wo_copy(d, k, other).start()
        wo_load(d).start()
        return carry

    lax.fori_loop(0, nz, start_wo, 0)

    mine = doc[...].astype(F32)
    last_doc = mine[7:8, 127:128]
    for i in range(8):
        row = mine[i : i + 1, :]
        docr[0:1, LEAD + i * 128 : LEAD + (i + 1) * 128] = row
        docc[i * 128 : (i + 1) * 128, :] = jnp.broadcast_to(row, (128, 128)).T

    for load in loads[1:]:
        load.wait()

    lag = 6

    def own_unit(u, what="both"):
        @pl.when(u >= n_sub)
        def _():
            ring_arrival(u).wait_recv()

            @pl.when(u < units - n_sub)
            def _():
                ring_copy(u).start()

            par_copy(u, k, way).start()

        accumulate(u, k, way, what)

    def partner_unit(u, what="both"):
        par_copy(u, other, -way).wait_recv()
        accumulate(u, other, -way, what)

    def ring_step(u, carry):
        own_unit(u)

        @pl.when(u >= lag)
        def _():
            partner_unit(u - lag)

        return carry

    turn = units - n_sub
    lax.fori_loop(0, 2 * n_sub, ring_step, 0)
    hear(0)
    tell(1)
    lax.fori_loop(2 * n_sub, 3 * n_sub, ring_step, 0)
    hear(1)
    tell(2)
    lax.fori_loop(3 * n_sub, turn, ring_step, 0)
    hear(2)

    def start_doc(n, carry):
        doc_copy(lax.rem(b + n, nctx), b).start()
        return carry

    lax.fori_loop(1, nctx, start_doc, 0)

    one_k, two_k = factor_bias((PACKED, 1), 0)

    def finish(i):
        rows = sub_rows(i)
        late = pl.ds(pl.multiple_of(LEAD + i * SUB, 128), SUB)
        x = af[rows, :].astype(BF16)
        v = av[rows, :].astype(BF16)
        feat[rows, :] = x
        vcat[late, :] = v
        keeps = docr[0:1, late] == last_doc
        for j in range(2):
            at = 256 + 2 * PACKED * j
            left = dot_nt(table[at : at + PACKED, 0:64], x) + one_k
            right = dot_nt(table[at + PACKED : at + 2 * PACKED, 0:64], x) + two_k
            phi_k = jnp.where(keeps, left * right, 0.0).astype(BF16)
            st_acc[j] += dot(phi_k, v[:, j * 128 : (j + 1) * 128])

    def catch_up(n, carry):
        own_unit(turn + n)

        def partner_next(m, inner):
            partner_unit(turn - lag + 3 * n + m)
            return inner

        lax.fori_loop(0, 3, partner_next, 0)
        return carry

    def finish_early(n, carry):
        own_unit(turn + 2 + n, "state")
        partner_unit(turn + n, "state")
        finish(n)
        return carry

    def finish_late(n, carry):
        partner_unit(turn + 2 + n, "state")
        finish(2 + n)
        return carry

    lax.fori_loop(0, 2, catch_up, 0)
    lax.fori_loop(0, 2, finish_early, 0)
    lax.fori_loop(0, 2, finish_late, 0)

    def tail_copy(n):
        buf = (kcat, vcat)[n]
        return pltpu.make_async_remote_copy(
            src_ref=buf.at[LEAD + rows_total - WIN : LEAD + rows_total],
            dst_ref=buf.at[LEAD - WIN : LEAD],
            send_sem=tail_send.at[n],
            recv_sem=tail_recv.at[n],
            device_id={"ctx": lax.rem(b + 1, nctx)},
            device_id_type=MESH,
        )

    for j in range(2):
        st_send[:, j * part : (j + 1) * part, :] = st_acc[j].astype(BF16).reshape(owners, part, 128)

    def st_copy(c, slot):
        return pltpu.make_async_remote_copy(
            src_ref=st_send.at[c],
            dst_ref=st_recv.at[slot],
            send_sem=st_ssem.at[0],
            recv_sem=st_rsem.at[0],
            device_id={"ctx": c},
            device_id_type=MESH,
        )

    def start_state(c):
        @pl.when(c < owners)
        def _():
            st_copy(c, b).start()

    for n in far_first:
        start_state(lax.rem(b + n, nctx))

    def window_rows(i, carry):
        rows = sub_rows(i)
        late = pl.ds(pl.multiple_of(LEAD + i * SUB, 128), SUB)
        wq[rows, 0:128] = aw[rows, 0:128].astype(BF16)
        kcat[late, 0:128] = aw[rows, 128:256].astype(BF16)
        wq[rows, 128:256] = aw[rows, 256:384].astype(BF16)
        kcat[late, 128:256] = aw[rows, 384:512].astype(BF16)
        return carry

    def window_late(n, carry):
        accumulate(turn + 2 + n, k, way, "window")
        accumulate(turn + n, other, -way, "window")
        accumulate(turn + 2 + n, other, -way, "window")
        return carry

    lax.fori_loop(0, 2, window_late, 0)
    lax.fori_loop(0, n_sub, window_rows, 0)

    @pl.when(b < nctx - 1)
    def _():
        tail_copy(0).start()
        tail_copy(1).start()

    def feature_rows(i, carry):
        rows = sub_rows(i)
        x = feat[rows, :]
        for j in range(2):
            at = 896 + 64 * j
            fq[j, rows, :] = dot(x, table[at : at + 64, 0:64]).astype(BF16)
        return carry

    lax.fori_loop(0, n_sub, feature_rows, 0)

    def taylor_rows(i):
        lo, hi = i * SUB, (i + 1) * SUB
        t_pos = lax.broadcasted_iota(jnp.int32, (SUB, hi), 0) + lo
        s_pos = lax.broadcasted_iota(jnp.int32, (SUB, hi), 1)
        allowed = (s_pos <= t_pos) & (docc[lo:hi, 0:1] == docr[0:1, LEAD : LEAD + hi])
        for j in range(2):
            d = dot_nt(fq[j, lo:hi, :], feat[0:hi, :])
            taylor = jnp.where(allowed, 1.0 + d * (0.25 + d * 0.03125), 0.0).astype(BF16)
            lin[lo:hi, j * 128 : (j + 1) * 128] = dot(
                taylor, vcat[LEAD : LEAD + hi, j * 128 : (j + 1) * 128]
            )

    taylor_rows(0)
    taylor_rows(1)

    def sum_back(c, slot):
        return pltpu.make_async_remote_copy(
            src_ref=st_sums.at[c],
            dst_ref=st.at[slot],
            send_sem=sum_ssem.at[0],
            recv_sem=sum_rsem.at[0],
            device_id={"ctx": c},
            device_id_type=MESH,
        )

    bulk(docs.at[0 : nctx - 1], doc_recv).wait()
    docs[b] = doc[...]

    def start_sum(c):
        @pl.when(c > 0)
        def _():
            sum_back(c, b).start()

    @pl.when(b < owners)
    def _():
        bulk(st_recv.at[0 : nctx - 1], st_rsem).wait()
        st_recv[b] = st_send[b]
        sums = jnp.zeros((2 * part, 128), F32)
        for c in range(nctx - 1):
            same = docs[c][7:8, 127:128] == docs[max(c - 1, 0)][7:8, 127:128]
            sums = st_recv[c].astype(F32) + jnp.where(same, sums, 0.0)
            st_sums[c + 1] = sums.astype(BF16)
        for n in far_first:
            start_sum(lax.rem(b + n, nctx))

    one_q, two_q = factor_bias((1, WIDE), 1)

    def query_rows(i, carry):
        rows = sub_rows(i)
        x = feat[rows, :]
        for j in range(2):
            left = dot(x, table[128 * j : 128 * j + 64, :]) + one_q
            right = dot(x, table[128 * j + 64 : 128 * j + 128, :]) + two_q
            phiq[j, rows, :] = (left * right).astype(BF16)
        return carry

    lax.fori_loop(0, n_sub, query_rows, 0)
    taylor_rows(2)
    taylor_rows(3)

    @pl.when(b == 0)
    def _():
        docr[0:1, 0:LEAD] = jnp.full((1, LEAD), -1.0, F32)

    @pl.when(b > 0)
    def _():
        tail_copy(0).wait_recv()
        tail_copy(1).wait_recv()
        docr[0:1, 0:LEAD] = docs[b - 1][7:8, :].astype(F32)

    tile, reach = 128, LEAD + 128
    gap = lax.broadcasted_iota(jnp.int32, (tile, reach), 1) - lax.broadcasted_iota(
        jnp.int32, (tile, reach), 0
    )
    band = (gap > LEAD - WIN) & (gap <= LEAD)
    for i in range(rows_total // tile):
        lo, hi = i * tile, (i + 1) * tile
        within = band & (docc[lo:hi, 0:1] == docr[0:1, lo : lo + reach])
        for j in range(2):
            at = slice(j * 128, (j + 1) * 128)
            logits = jnp.where(within, dot_nt(wq[lo:hi, at], kcat[lo : lo + reach, at]), -1e30)
            top = jnp.max(logits, -1, keepdims=True)
            weights = jnp.exp((logits - top) * HEAD_DIM ** (-0.5))
            probs = (weights * (1.0 / jnp.sum(weights, -1, keepdims=True))).astype(BF16)
            win[lo:hi, at] = dot(probs, vcat[lo : lo + reach, at])

    @pl.when(b == 0)
    def _():
        st[...] = jnp.zeros_like(st)

    @pl.when((b > 0) & (b < owners))
    def _():
        bulk(st.at[0 : owners - 1], sum_rsem).wait()
        st[b] = st_sums[b]

    @pl.when((b > 0) & (b >= owners))
    def _():
        bulk(st, sum_rsem).wait()

    rest = jnp.zeros((WIDE - PACKED, 128), BF16)
    state = [
        jnp.concatenate([st[:, j * part : (j + 1) * part, :].reshape(PACKED, 128), rest], 0)
        for j in range(2)
    ]

    def mix_copy(i, side):
        slot = mix.at[side, sub_rows(i)]
        return pltpu.make_async_remote_copy(
            src_ref=slot,
            dst_ref=slot,
            send_sem=mix_send.at[0],
            recv_sem=mix_recv.at[i],
            device_id={"head": partner},
            device_id_type=MESH,
        )

    def mix_rows(i, carry):
        rows = sub_rows(i)
        uses = docc[rows, :] == docr[0:1, LEAD - 1 : LEAD]
        for j in range(2):
            at = slice(j * 128, (j + 1) * 128)
            carried = dot(phiq[j, rows, :], state[j])
            linear = lin[rows, at] + jnp.where(uses, carried, 0.0)
            square = jnp.mean(linear * linear, -1, keepdims=True)
            normed = linear * lax.rsqrt(square + 1e-5)
            mix[k, rows, at] = (normed + win[rows, at]).astype(BF16)
        mix_copy(i, k).start()
        return carry


    bulk(wo.at[k], wo_sem).wait()
    bulk(wo.at[other], wo_recv).wait()

    def sum_copy(u):
        s = u // n_sub
        i = u - s * n_sub
        return pltpu.make_async_remote_copy(
            src_ref=sbuf.at[s, i],
            dst_ref=rbuf.at[s, i],
            send_sem=rs_send.at[0],
            recv_sem=rs_recv.at[u],
            device_id={"head": ahead},
            device_id_type=MESH,
        )

    def sum_step(u, carry):
        s = u // n_sub
        i = u - s * n_sub
        rows = sub_rows(i)
        dest = lax.rem(z - (s + 1) * way + 2 * nz, nz)

        @pl.when(u < n_sub)
        def _():
            mix_copy(i, other).wait_recv()

        part = dot(mix[0, rows, :], wo[0, dest]) + dot(mix[1, rows, :], wo[1, dest])

        @pl.when(u < n_sub)
        def _():
            sbuf[s, i] = part.astype(BF16)
            sum_copy(u).start()

        @pl.when(u >= n_sub)
        def _():
            sum_copy(u - n_sub).wait_recv()
            both = (part + rbuf[s - 1, i].astype(F32)).astype(BF16)

            @pl.when(u < units - n_sub)
            def _():
                sbuf[s, i] = both
                sum_copy(u).start()

            @pl.when(u >= units - n_sub)
            def _():
                out[rows, :] = both

        return carry

    def first_step(i, carry):
        @pl.when(i < n_sub)
        def _():
            mix_rows(i, 0)

        @pl.when(i > 0)
        def _():
            sum_step(i - 1, 0)

        return carry

    lax.fori_loop(0, n_sub + 1, first_step, 0)
    lax.fori_loop(n_sub, units, sum_step, 0)

    bulk(gath.at[k, 0 : nz - 1], ring_send).wait()
    bulk(gath.at[k], par_send).wait()
    bulk(sbuf, rs_send).wait()
    bulk(docs.at[0 : nctx - 1], doc_send).wait()
    bulk(mix.at[k], mix_send).wait()
    bulk(wo.at[k], wo_send).wait()

    @pl.when(b < owners)
    def _():
        bulk(st_send.at[0 : owners - 1], st_ssem).wait()

    @pl.when(b >= owners)
    def _():
        bulk(st_send, st_ssem).wait()

    @pl.when(b == 0)
    def _():
        bulk(st_sums.at[0 : nctx - 1], sum_ssem).wait()

    @pl.when((b > 0) & (b < owners))
    def _():
        bulk(st_sums.at[0 : nctx - 2], sum_ssem).wait()

    @pl.when(b < nctx - 1)
    def _():
        tail_copy(0).wait_send()
        tail_copy(1).wait_send()


def solution(mesh):
    nctx, nhead = mesh.shape["ctx"], mesh.shape["head"]
    nz = nhead // 2

    def shards(tokens, doc_ids, w_feat, w_value, w_window, w_out):
        rows = tokens.shape[0]
        width = w_value.shape[0]
        n_sub = rows // SUB
        units = n_sub * nz
        owners = min(nctx, 10)
        dma = pltpu.SemaphoreType.DMA
        vmem = pltpu.VMEM
        hbm_space = pl.BlockSpec(memory_space=pltpu.HBM)
        vmem_space = pl.BlockSpec(memory_space=pltpu.VMEM)
        return pl.pallas_call(
            functools.partial(kernel, nctx, nz),
            out_shape=jax.ShapeDtypeStruct((rows, 256), BF16),
            in_specs=[hbm_space] * 7,
            out_specs=vmem_space,
            scratch_shapes=[
                vmem((8, 128), jnp.int32),
                vmem((2, nz, rows, 256), BF16),
                vmem((64, width), BF16),
                vmem((width, 256), BF16),
                vmem((width, 512), BF16),
                vmem((rows, 64), F32),
                vmem((rows, 256), F32),
                vmem((rows, 512), F32),
                vmem((TABLE, WIDE), BF16),
                vmem((rows, 64), BF16),
                vmem((rows, 256), BF16),
                vmem((LEAD + rows, 256), BF16),
                vmem((LEAD + rows, 256), BF16),
                vmem((rows, 128), F32),
                vmem((1, LEAD + rows), F32),
                vmem((2, rows, 64), BF16),
                vmem((2, rows, WIDE), BF16),
                vmem((nctx, 8, 128), jnp.int32),
                vmem((rows, 256), F32),
                vmem((rows, 256), F32),
                vmem((2, PACKED, 128), F32),
                vmem((owners, 2 * PACKED // owners, 128), BF16),
                vmem((nctx, 2 * PACKED // owners, 128), BF16),
                vmem((nctx, 2 * PACKED // owners, 128), BF16),
                vmem((owners, 2 * PACKED // owners, 128), BF16),
                vmem((2, rows, 256), BF16),
                vmem((2, nz, 256, 256), BF16),
                vmem((nz - 1, n_sub, SUB, 256), BF16),
                vmem((nz - 1, n_sub, SUB, 256), BF16),
                dma((5,)),
                dma((n_sub,)),
                dma((1,)),
                dma((1,)),
                dma((units,)),
                dma((1,)),
                dma((units,)),
                dma((1,)),
                dma((1,)),
                dma((1,)),
                dma((1,)),
                dma((1,)),
                dma((1,)),
                dma((1,)),
                dma((1,)),
                dma((2,)),
                dma((2,)),
                dma((1,)),
                dma((n_sub,)),
                dma((1,)),
                dma((units - n_sub,)),
                pltpu.SemaphoreType.REGULAR((3,)),
            ],
            compiler_params=pltpu.CompilerParams(
                collective_id=0, has_side_effects=True, vmem_limit_bytes=67043328 - 11000 * 1024
            ),
            name="based_layer",
        )(
            tokens,
            pltpu.with_memory_space_constraint(doc_ids.reshape(8, 128), pltpu.HBM),
            w_feat.T,
            w_value,
            w_window,
            w_out,
            selection_tables(),
        )

    return jax.shard_map(
        shards,
        mesh=mesh,
        in_specs=(
            P("ctx", "head"),
            P("ctx"),
            P(None, "head"),
            P(None, "head"),
            P(None, "head"),
            P("head", None),
        ),
        out_specs=P("ctx", "head"),
        check_vma=False,
    )
```
